32 devices in a mesh: rep: 8 (over y, x, core), shard: 4 (over z).
Axes of the slice: x: 2, y: 2, z: 4, core: 2. Of those that a mesh axis runs over, the one named last changes fastest.
Arguments:
- tokens: bfloat16 [64, 256, 1024], P('rep', 'shard'), may hold values from -6 to 6
- cotangent: bfloat16 [64, 256, 1024], P('rep', 'shard'), may hold values from -6 to 6
- lengths: int32 [8, 8], P('rep'), may hold values from 1 to 256, 1280 in all within a row
- factor_weight: bfloat16 [1024, 800], P('shard'), may hold values from -0.25 to 0.25
- out_weight: bfloat16 [1024, 1024], P('shard'), may hold values from -0.75 to 0.75
- gate_weight: bfloat16 [1024, 2816], P('shard'), may hold values from -0.1875 to 0.1875
- up_weight: bfloat16 [1024, 2816], P('shard'), may hold values from -0.1875 to 0.1875
- down_weight: bfloat16 [2816, 1024], P('shard'), may hold values from -0.109375 to 0.109375
- first_gain: bfloat16 [1024], P('shard'), may hold values from 0.5 to 1.5
- second_gain: bfloat16 [1024], P('shard'), may hold values from 0.5 to 1.5
Outputs:
- output: bfloat16 [64, 256, 1024], P('rep', 'shard')
- input_grad: bfloat16 [64, 256, 1024], P('rep', 'shard')
- factor_grad: float32 [1024, 800], P('shard')
- out_grad: float32 [1024, 1024], P('shard')
- gate_grad: float32 [1024, 2816], P('shard')
- up_grad: float32 [1024, 2816], P('shard')
- down_grad: float32 [2816, 1024], P('shard')
- first_grad: float32 [1024], P('shard')
- second_grad: float32 [1024], P('shard')
The draws below stay inside these ranges and needn't reach their ends.
Inputs may be any that keep to these rules, and one draw needn't show every extreme that they name: Row g holds the lengths of sequences g * 8 to g * 8 + 7; each row sums to 1280 and holds 256 at least once.
All inputs are finite; a program needn't handle non-finite values.
Results may differ from the reference program's by a relative error of at most 0.02.
The reference program's roundings to bfloat16 on the way count: a program that leaves them out, or rounds other values in their place, can miss the bound.
Values may be sent and summed in bfloat16 or wider, within the bound.
No kernel may reach another device: no remote copies, remote signals or barrier semaphores. Data moves between devices by JAX's collectives and lax.ppermute only.
A program may use at most 192 MiB of HBM per device.

```python
import math
import jax
import jax.numpy as jnp
import numpy as np
from jax import lax

D = 1024
H = 16
DH = 64
RQ = 6
RK = 2
FF = 2816
SEQ_MAX = 256
SEQ_GROUP = 8
GROUPS = 8
SEQS = 64
FACTORS = 800
N_SHARD = 4


def steps_of(key, extent, pieces, low, largest):
    def one(dim, parts):
        steps = jax.random.uniform(jax.random.fold_in(jax.random.fold_in(key, 6), dim), (parts,), jnp.float32, low / len(pieces), largest / len(pieces))
        return jnp.repeat(jnp.exp(steps), extent[dim] // parts).reshape((-1,) + (1,) * (len(extent) - dim - 1))

    gain = one(*pieces[0])
    for cut in pieces[1:]:
        gain = gain * one(*cut)
    return gain


def length_profile(count, total, reach, skew):
    portions = [(1 << 20) // math.isqrt(grade ** skew) + 1 for grade in range(2, count + 1)]
    rest, holding = total - reach - (count - 1), [1] * (count - 1)
    while rest > 0:
        free = [i for i in range(count - 1) if holding[i] < reach]
        pool, left = sum([portions[i] for i in free]), rest
        for i in free:
            addition = min(reach - holding[i], max(1, left * portions[i] // pool), rest)
            holding[i] = holding[i] + addition
            rest = rest - addition
    return np.array([reach] + holding)


def uneven(key, count, total, limit, skew):
    if count == 2:
        one = jax.random.randint(key, (), max(1, total - limit), min(limit, total - 1) + 1)
        return jnp.stack([one, total - one])
    sizes = jnp.asarray(length_profile(count, total, limit, skew), jnp.int32)
    pairs = (count - 1) // 2
    giver, receiver = sizes[1:1 + 2 * pairs:2], sizes[2:2 + 2 * pairs:2]
    slack = jnp.minimum(giver - 1, limit - receiver)
    moved = jax.random.randint(jax.random.fold_in(key, 1), (pairs,), 0, 1 << 20) % (slack + 1)
    sizes = sizes.at[1:1 + 2 * pairs:2].set(giver - moved).at[2:2 + 2 * pairs:2].set(receiver + moved)
    return sizes[jax.random.permutation(jax.random.fold_in(key, 2), count)]


def scatter_about(rng, dims, width, most, cuts=(), kind=jnp.bfloat16):
    drawn = width * jax.random.normal(rng, dims, jnp.float32)
    if cuts:
        drawn = drawn * steps_of(rng, dims, cuts, -0.22, 0.18)
    return jnp.clip(drawn, -most, most).astype(kind)


def setup_inputs(seed: int = 0) -> dict:
    splits = jax.random.split(jax.random.key(seed), 11)
    return {
        "tokens": scatter_about(splits[0], (SEQS, SEQ_MAX, D), 1.0, 6.0, ((0, 8), (1, 4))),
        "cotangent": scatter_about(splits[1], (SEQS, SEQ_MAX, D), 1.0, 6.0, ((0, 8), (1, 4))),
        "lengths": jax.vmap(lambda own: uneven(own, SEQ_GROUP, SEQ_GROUP * SEQ_MAX * 5 // 8, SEQ_MAX, 2))(jax.random.split(splits[2], GROUPS)).reshape((GROUPS, SEQ_GROUP)).astype(jnp.int32),
        "factor_weight": scatter_about(splits[3], (D, FACTORS), (D // 2) ** -0.5, 0.25, ((0, 4),)),
        "out_weight": scatter_about(splits[4], (H * DH, D), (D // 16) ** -0.5, 0.75, ((0, 4),)),
        "gate_weight": scatter_about(splits[5], (D, FF), D ** -0.5, 0.1875, ((0, 4),)),
        "up_weight": scatter_about(splits[6], (D, FF), D ** -0.5, 0.1875, ((0, 4),)),
        "down_weight": scatter_about(splits[7], (FF, D), FF ** -0.5, 0.109375, ((0, 4),)),
        "first_gain": jnp.clip(1.0 + 0.1 * jax.random.normal(splits[8], (D,), jnp.float32), 0.5, 1.5).astype(jnp.bfloat16),
        "second_gain": jnp.clip(1.0 + 0.1 * jax.random.normal(splits[9], (D,), jnp.float32), 0.5, 1.5).astype(jnp.bfloat16),
    }


@jax.custom_vjp
def low(v):
    return lax.optimization_barrier(v.astype(jnp.bfloat16)).astype(jnp.float32)

@jax.custom_vjp
def low_back(v):
    return v

def low_keep(v):
    return (low(v), None)

def low_pass(kept, grad):
    return (grad,)

def back_keep(v):
    return (v, None)

def back_low(kept, grad):
    return (low(grad),)
low.defvjp(low_keep, low_pass)
low_back.defvjp(back_keep, back_low)
EPSILON = 1e-06
PRECISE = lax.Precision.HIGHEST

def normalize(inputs, gain_full):
    return inputs * lax.rsqrt(lax.optimization_barrier(jnp.mean(inputs * inputs, axis=-1, keepdims=True)) + EPSILON) * gain_full

def rotary_tables(seq_length):
    position = jnp.arange(seq_length).astype(jnp.float32)
    freq = jnp.exp(jnp.arange(DH // 2).astype(jnp.float32) * (-2.0 * math.log(10000.0) / DH))
    angle = position[:, None] * freq[None, :]
    return (jnp.cos(angle)[:, None, :], jnp.sin(angle)[:, None, :])

def rotate(vector, cosine, sine_part, direction):
    half_size = vector.shape[-1] // 2
    first_half = vector[..., :half_size]
    second_half = vector[..., half_size:]
    return jnp.concatenate([first_half * cosine - direction * second_half * sine_part, second_half * cosine + direction * first_half * sine_part], axis=-1)

def compose(factors, cosine, sine_part):
    lead = factors.shape[:-1]
    edge_one = RQ * H
    edge_two = edge_one + RK * H
    edge_three = edge_two + RK * H
    edge_four = edge_three + RQ * DH
    edge_five = edge_four + RK * DH
    query_heads = factors[..., :edge_one].reshape(lead + (RQ, H))
    key_heads = factors[..., edge_one:edge_two].reshape(lead + (RK, H))
    value_heads = factors[..., edge_two:edge_three].reshape(lead + (RK, H))
    query_dims = rotate(factors[..., edge_three:edge_four].reshape(lead + (RQ, DH)), cosine, sine_part, 1.0)
    key_dims = rotate(factors[..., edge_four:edge_five].reshape(lead + (RK, DH)), cosine, sine_part, 1.0)
    value_dims = factors[..., edge_five:].reshape(lead + (RK, DH))
    queries = jnp.einsum('...rh,...re->...he', query_heads, query_dims, precision=PRECISE) / RQ
    key_rows = jnp.einsum('...rh,...re->...he', key_heads, key_dims, precision=PRECISE) / RK
    values = jnp.einsum('...rh,...re->...he', value_heads, value_dims, precision=PRECISE) / RK
    return (queries, key_rows, values)

def layer_forward(inputs, live_rows, factor_weight, out_weight, gate_weight, up_weight, down_weight, first_gain, second_gain):
    seq_count, seq_length, model_width = inputs.shape
    cosine, sine_part = rotary_tables(seq_length)
    first_low = low(normalize(inputs, first_gain))
    factors = low_back(jnp.einsum('bld,dc->blc', first_low, factor_weight, precision=PRECISE))
    queries, key_rows, values = compose(factors, cosine, sine_part)
    queries = low(queries)
    key_rows = low(key_rows)
    values = low(values)
    scores = low_back(jnp.einsum('bthe,buhe->bhtu', queries, key_rows, precision=PRECISE) * DH ** (-0.5))
    position = jnp.arange(seq_length)
    allowed = (position[None, :] <= position[:, None])[None, None] & live_rows[:, None, None, :]
    scores = jnp.where(allowed, scores, -1e+30)
    soft_low = low(jax.nn.softmax(scores, axis=-1))
    attended = low_back(low(jnp.einsum('bhtu,buhe->bthe', soft_low, values, precision=PRECISE)))
    attended = attended.reshape(seq_count, seq_length, H * DH)
    middle = inputs + low_back(jnp.einsum('blk,kd->bld', attended, out_weight, precision=PRECISE))
    second_low = low(normalize(middle, second_gain))
    gate_pre = low_back(jnp.einsum('bld,df->blf', second_low, gate_weight, precision=PRECISE))
    up_pre = low_back(jnp.einsum('bld,df->blf', second_low, up_weight, precision=PRECISE))
    hidden = low(jax.nn.silu(gate_pre) * up_pre)
    result = middle + low_back(jnp.einsum('blf,fd->bld', hidden, down_weight, precision=PRECISE))
    return jnp.where(live_rows[..., None], result, 0.0)

def reference(tokens, cotangent, lengths, factor_weight, out_weight, gate_weight, up_weight, down_weight, first_gain, second_gain):
    step_count = tokens.shape[0] // N_SHARD
    inputs = tokens.astype(jnp.float32).reshape(step_count, N_SHARD, SEQ_MAX, D)
    upstream = cotangent.astype(jnp.float32).reshape(step_count, N_SHARD, SEQ_MAX, D)
    seq_lengths = lengths.reshape(step_count, N_SHARD)
    params = tuple((weight_item.astype(jnp.float32) for weight_item in (factor_weight, out_weight, gate_weight, up_weight, down_weight, first_gain, second_gain)))

    def one_step(carry, item):
        step_inputs, step_upstream, step_lengths = item
        live_rows = jnp.arange(SEQ_MAX)[None, :] < step_lengths[:, None]

        def forward(inputs_now, *weights_now):
            return layer_forward(inputs_now, live_rows, *weights_now)
        result, pullback = jax.vjp(forward, step_inputs, *params)
        grads = pullback(step_upstream)
        carry = jax.tree.map(jnp.add, carry, tuple(grads[1:]))
        return (carry, (result.astype(jnp.bfloat16), grads[0].astype(jnp.bfloat16)))
    start = tuple((jnp.zeros(weight_item.shape, jnp.float32) for weight_item in params))
    totals, (outputs, input_grads) = lax.scan(one_step, start, (inputs, upstream, seq_lengths))
    return (outputs.reshape(tokens.shape[0], SEQ_MAX, D), input_grads.reshape(tokens.shape[0], SEQ_MAX, D), totals[0], totals[1], totals[2], totals[3], totals[4], totals[5], totals[6])
```

```python
import math

import jax
import jax.numpy as jnp
from jax import lax
from jax.experimental import pallas as pl
from jax.experimental.pallas import tpu as pltpu
from jax.sharding import PartitionSpec as P

H = 16
DH = 64
RQ = 6
RK = 2


EPSILON = 1e-06
PRECISE = lax.Precision.HIGHEST


def normalize(inputs, gain_full):
    return (
        inputs * lax.rsqrt(jnp.mean(inputs * inputs, axis=-1, keepdims=True) + EPSILON) * gain_full
    )


def rotary_tables(seq_length):
    position = lax.iota(jnp.float32, seq_length)
    freq = jnp.exp(lax.iota(jnp.float32, DH // 2) * (-2.0 * math.log(10000.0) / DH))
    angle = position[:, None] * freq[None, :]
    return (jnp.cos(angle)[:, None, :], jnp.sin(angle)[:, None, :])


def rotate(vector, cosine, sine_part, direction):
    half_size = vector.shape[-1] // 2
    first_half = vector[..., :half_size]
    second_half = vector[..., half_size:]
    return jnp.concatenate(
        [
            first_half * cosine - direction * second_half * sine_part,
            second_half * cosine + direction * first_half * sine_part,
        ],
        axis=-1,
    )


def compose(factors, cosine, sine_part):
    lead = factors.shape[:-1]
    edge_one = RQ * H
    edge_two = edge_one + RK * H
    edge_three = edge_two + RK * H
    edge_four = edge_three + RQ * DH
    edge_five = edge_four + RK * DH
    query_heads = factors[..., :edge_one].reshape(lead + (RQ, H))
    key_heads = factors[..., edge_one:edge_two].reshape(lead + (RK, H))
    value_heads = factors[..., edge_two:edge_three].reshape(lead + (RK, H))
    query_dims = rotate(
        factors[..., edge_three:edge_four].reshape(lead + (RQ, DH)), cosine, sine_part, 1.0
    )
    key_dims = rotate(
        factors[..., edge_four:edge_five].reshape(lead + (RK, DH)), cosine, sine_part, 1.0
    )
    value_dims = factors[..., edge_five:].reshape(lead + (RK, DH))
    queries = jnp.einsum("...rh,...re->...he", query_heads, query_dims, precision=PRECISE) / RQ
    key_rows = jnp.einsum("...rh,...re->...he", key_heads, key_dims, precision=PRECISE) / RK
    values = jnp.einsum("...rh,...re->...he", value_heads, value_dims, precision=PRECISE) / RK
    return (queries, key_rows, values)


AXES = {"x": (2, 1), "y": (4, 2), "c": (1, 4)}
PIECES = 8


def bit_of(axis):
    return (lax.axis_index("rep") // AXES[axis][0]) % 2


def swap(value, axis):
    step = AXES[axis][0]
    return lax.ppermute(value, "rep", [(i, i ^ step) for i in range(lax.axis_size("rep"))])


def onward(value):
    count = lax.axis_size("shard")
    return lax.ppermute(value, "shard", [(i, (i + 1) % count) for i in range(count)])


def piece_rows(rows, by_columns):
    return rows // (PIECES // 2) if by_columns else rows // PIECES


def own_piece(shard, by_columns):
    rows, columns = shard.shape
    quarter = bit_of("y") * 2 + bit_of("x")
    core = bit_of("c")
    size = piece_rows(rows, by_columns)
    if by_columns:
        return lax.dynamic_slice(shard, (quarter * size, core * (columns // 2)), (size, columns // 2))
    return lax.dynamic_slice(shard, ((core * 4 + quarter) * size, 0), (size, columns))


def assemble(shard, parts, by_columns):
    count = lax.axis_size("shard")
    rows, columns = shard.shape
    size, width = parts[0][1].shape[2:]
    where = lax.axis_index("shard")
    mine = bit_of("c") * 4 + bit_of("y") * 2 + bit_of("x")
    masks = [mask for group, _ in parts for mask in group]
    if size % 8 or rows % 8:
        stacked = jnp.concatenate([array for _, array in parts], axis=0)
        place = jnp.zeros((PIECES,), jnp.int32).at[jnp.array(masks)].set(jnp.arange(PIECES))
        ordered = jnp.take(stacked, place[mine ^ jnp.arange(PIECES)], axis=0)
        ordered = ordered[:, (where - jnp.arange(count) - 1) % count % (count - 1)]
        if by_columns:
            ordered = ordered.reshape(2, 4, count, size, width).transpose(2, 1, 3, 0, 4)
        else:
            ordered = ordered.reshape(PIECES, count, size, width).transpose(1, 0, 2, 3)
        ordered = ordered.reshape(count, rows, columns)
        own = (jnp.arange(count) == where)[:, None, None]
        return jnp.where(own, shard[None], ordered).reshape(count * rows, columns)

    def kernel(place_ref, shard_ref, *refs):
        part_refs, out_ref, sems = refs[: len(parts)], refs[len(parts)], refs[len(parts) + 1]
        here, piece = place_ref[0], place_ref[1]
        copies = [
            pltpu.make_async_copy(
                shard_ref, out_ref.at[pl.ds(pl.multiple_of(here * rows, 8), rows), :], sems.at[0]
            )
        ]
        for (group, _), ref in zip(parts, part_refs):
            for slot, mask in enumerate(group):
                target = piece ^ mask
                for step in range(1, count):
                    source = lax.rem(here - step + count, count)
                    if by_columns:
                        row = source * rows + lax.rem(target, 4) * size
                        column = pl.ds(pl.multiple_of((target // 4) * width, 128), width)
                    else:
                        row = source * rows + target * size
                        column = slice(None)
                    copies.append(
                        pltpu.make_async_copy(
                            ref.at[slot, step - 1],
                            out_ref.at[pl.ds(pl.multiple_of(row, 8), size), column],
                            sems.at[len(copies)],
                        )
                    )
        for copy in copies:
            copy.start()
        for copy in copies:
            copy.wait()

    total = 1 + PIECES * (count - 1)
    return pl.pallas_call(
        kernel,
        out_shape=jax.ShapeDtypeStruct((count * rows, columns), shard.dtype),
        in_specs=[pl.BlockSpec(memory_space=pltpu.SMEM)]
        + [pl.BlockSpec(memory_space=pl.ANY)] * (1 + len(parts)),
        out_specs=pl.BlockSpec(memory_space=pltpu.VMEM),
        scratch_shapes=[pltpu.SemaphoreType.DMA((total,))],
        name="assemble",
        cost_estimate=pl.CostEstimate(
            flops=0, transcendentals=0, bytes_accessed=2 * 2 * count * rows * columns
        ),
    )(jnp.stack([where, mine]).astype(jnp.int32), shard, *[array for _, array in parts])


def gather_weight(shard, order, by_columns=False):
    first, second = order
    piece = own_piece(shard, by_columns)
    ring = []
    for _ in range(lax.axis_size("shard") - 1):
        piece = onward(piece)
        ring.append(piece)
    ring = jnp.stack(ring)
    one = jnp.stack([ring, swap(ring, first)])
    two = swap(one, second)
    a, b, c = AXES[first][1], AXES[second][1], AXES["c"][1]
    parts = (
        ((0, a), one),
        ((b, a | b), two),
        ((c, c | a), swap(one, "c")),
        ((c | b, c | a | b), swap(two, "c")),
    )
    return assemble(shard, parts, by_columns)


def pick(value, index, axis):
    return lax.dynamic_index_in_dim(value, index, axis, keepdims=False)


def core_halves(value, blocks):
    width = value.shape[-1] // blocks // 2
    low = [value[:, (2 * j) * width : (2 * j + 1) * width] for j in range(blocks)]
    high = [value[:, (2 * j + 1) * width : (2 * j + 2) * width] for j in range(blocks)]
    low = jnp.concatenate(low, axis=-1)
    high = jnp.concatenate(high, axis=-1)
    second = bit_of("c") == 1
    return jnp.where(second, high, low), jnp.where(second, low, high)


def outer(left, right):
    return lax.dot_general(left, right, (((0,), (0,)), ((), ())), preferred_element_type=jnp.float32)


def sum_gradient(left, right, order, by_columns=False):
    count = lax.axis_size("shard")
    low = jnp.bfloat16
    if by_columns:
        keep, send = outer(left, right[0]), outer(left, right[1])
    else:
        keep, send = outer(left[0], right), outer(left[1], right)
    got = swap(send.astype(low), "c")
    total = (keep + got.astype(jnp.float32)).astype(low)
    rows, width = total.shape
    size = rows // count // 4
    total = total.reshape(count, 2, 2, size, width)
    dims = {"y": 1, "x": 2}
    first, second = order
    for axis, dim in ((first, dims[first]), (second, 1)):
        other = pick(total, 1 - bit_of(axis), dim)
        got = swap(other, axis)
        total = (pick(total, bit_of(axis), dim).astype(jnp.float32) + got.astype(jnp.float32)).astype(low)
    here = lax.axis_index("shard")
    part = pick(total, (here - 1) % count, 0)
    for step in range(1, count):
        part = onward(part)
        mine = pick(total, (here - 1 - step) % count, 0)
        part = (part.astype(jnp.float32) + mine.astype(jnp.float32)).astype(low)
    extra = lax.axis_size("rep") // PIECES
    if extra > 1:
        groups = [[i + PIECES * j for j in range(extra)] for i in range(PIECES)]
        part = lax.psum(part, "rep", axis_index_groups=groups)

    def both(value, axis, dim):
        got = swap(value, axis)
        second_half = bit_of(axis) == 1
        return jnp.stack(
            [jnp.where(second_half, got, value), jnp.where(second_half, value, got)], axis=dim
        )

    quarters = both(part, first, 0)
    quarters = both(quarters, second, 0 if second == "y" else 1)
    quarters = quarters.reshape(4 * size, width)
    whole = both(quarters, "c", 1 if by_columns else 0)
    whole = whole.reshape(4 * size, 2 * width) if by_columns else whole.reshape(8 * size, width)
    return whole.astype(jnp.float32)


def attention_of(factors, seq_length):
    row_count = factors.shape[0]
    positions = lax.iota(jnp.int32, row_count)
    live_rows = positions < seq_length
    cosine, sine_part = rotary_tables(row_count)
    score_scale = DH ** (-0.5)
    allowed = (positions[None, :] <= positions[:, None]) & live_rows[None, :]
    (queries, key_rows, values), compose_back = jax.vjp(
        lambda whole: compose(whole, cosine, sine_part), factors
    )
    queries = queries.astype(jnp.bfloat16)
    key_rows = key_rows.astype(jnp.bfloat16)
    values = values.astype(jnp.bfloat16)

    def scores_of():
        raw_scores = (
            jnp.einsum("the,uhe->htu", queries, key_rows, preferred_element_type=jnp.float32)
            * score_scale
        )
        return jnp.where(allowed[None], raw_scores, -1e30)

    scores = scores_of()
    row_max = jnp.max(scores, axis=-1, keepdims=True)
    shifted = jnp.exp(scores - row_max)
    row_total = jnp.sum(shifted, axis=-1, keepdims=True)
    log_total = row_max + jnp.log(row_total)
    probs_low = (shifted / row_total).astype(jnp.bfloat16)
    attended = jnp.einsum("htu,uhe->the", probs_low, values, preferred_element_type=jnp.float32)
    attended = attended.astype(jnp.bfloat16).reshape(row_count, H * DH)

    def back(attended_grad):
        attended_grad = attended_grad.reshape(row_count, H, DH)
        probs_full = jnp.exp(scores_of() - log_total)
        prob_grad = jnp.einsum(
            "the,uhe->htu", attended_grad, values, preferred_element_type=jnp.float32
        )
        row_delta = jnp.sum(probs_full * prob_grad, axis=-1, keepdims=True)
        score_grad = (probs_full * (prob_grad - row_delta)).astype(jnp.bfloat16)
        query_grad = (
            jnp.einsum("htu,uhe->the", score_grad, key_rows, preferred_element_type=jnp.float32)
            * score_scale
        )
        key_grad = (
            jnp.einsum("htu,the->uhe", score_grad, queries, preferred_element_type=jnp.float32)
            * score_scale
        )
        value_grad = jnp.einsum(
            "htu,the->uhe",
            probs_full.astype(jnp.bfloat16),
            attended_grad,
            preferred_element_type=jnp.float32,
        )
        (factor_full_grad,) = compose_back((query_grad, key_grad, value_grad))
        return factor_full_grad.astype(jnp.bfloat16)

    return attended, back


def matmul(left, right):
    return jnp.dot(left, right, preferred_element_type=jnp.float32)


def matmul_back(left, right):
    return lax.dot_general(left, right, (((1,), (1,)), ((), ())), preferred_element_type=jnp.float32)


def norm_scale(value):
    return lax.rsqrt(jnp.mean(value * value, axis=-1, keepdims=True) + EPSILON)


def norm_back(grad, gain, normed, scale):
    scaled = grad * gain
    return scale * (scaled - normed * jnp.mean(scaled * normed, axis=-1, keepdims=True))


def deal(value):
    groups = lax.axis_size("shard")
    batches = value.shape[0] // groups
    rows, width = value.shape[1:]
    dealt = lax.all_to_all(
        value.reshape(batches, groups, rows, width), "shard", split_axis=1, concat_axis=2, tiled=True
    )
    return dealt.reshape(batches * groups * rows, width)


def give_back(value, batches):
    groups = lax.axis_size("shard")
    width = value.shape[-1]
    home = lax.all_to_all(
        value.reshape(batches, 1, -1, width), "shard", split_axis=2, concat_axis=1, tiled=True
    )
    return home.reshape(batches * groups, -1, width)


def on_device(
    tokens,
    cotangent,
    lengths,
    factor_weight,
    out_weight,
    gate_weight,
    up_weight,
    down_weight,
    first_gain,
    second_gain,
):
    low = jnp.bfloat16
    groups = lax.axis_size("shard")
    batches = tokens.shape[0] // groups
    row_count = tokens.shape[1] * groups
    factor_count = factor_weight.shape[1]
    padded = -(-(factor_count + 2) // 128) * 128
    own_slot = lax.iota(jnp.int32, groups) == lax.axis_index("shard")
    own_lengths = jnp.sum(jnp.where(own_slot[None, :], lengths.reshape(batches, groups), 0), axis=1)
    live = (lax.iota(jnp.int32, row_count)[None, :] < own_lengths[:, None]).reshape(-1, 1)

    inputs = deal(tokens).astype(jnp.float32)
    shard = jnp.concatenate([factor_weight, first_gain[:, None], second_gain[:, None]], axis=1)
    shard = jnp.pad(shard, ((0, 0), (0, padded - factor_count - 2)))
    factor_full = gather_weight(shard, ("x", "y"))
    out_full = gather_weight(out_weight, ("x", "y"))
    gate_full = gather_weight(gate_weight, ("x", "y"))
    up_full = gather_weight(up_weight, ("y", "x"))
    down_full = gather_weight(down_weight, ("y", "x"), by_columns=True)
    upstream = jnp.where(live, deal(cotangent).astype(jnp.float32), 0.0)
    upstream_low = upstream.astype(low)

    at = lax.broadcasted_iota(jnp.int32, (8, padded), 1) - factor_count
    chosen = (at == lax.broadcasted_iota(jnp.int32, (8, padded), 0)).astype(low)
    gains = matmul_back(chosen, factor_full)
    gain_one, gain_two = gains[0:1], gains[1:2]

    scale_one = norm_scale(inputs)
    normed_one = inputs * scale_one
    first_low = (normed_one * gain_one).astype(low)
    factors = matmul(first_low, factor_full)
    pieces = [
        attention_of(factors[j * row_count : (j + 1) * row_count, :factor_count], own_lengths[j])
        for j in range(batches)
    ]
    attended = jnp.concatenate([piece[0] for piece in pieces], axis=0)
    middle = inputs + matmul(attended, out_full)
    scale_two = norm_scale(middle)
    normed_two = middle * scale_two
    second_low = (normed_two * gain_two).astype(low)
    gate_pre = matmul(second_low, gate_full)
    up_pre = matmul(second_low, up_full)
    sigmoid = jax.nn.sigmoid(gate_pre)
    hidden = (gate_pre * sigmoid * up_pre).astype(low)
    result = middle + matmul(hidden, down_full)
    output = jnp.where(live, result, 0.0).astype(low)
    home_output = give_back(output, batches)

    down_grad = sum_gradient(hidden, core_halves(upstream_low, 1), ("y", "x"), by_columns=True)
    hidden_grad = matmul_back(upstream_low, down_full)
    gate_low = (hidden_grad * up_pre * sigmoid * (1.0 + gate_pre * (1.0 - sigmoid))).astype(low)
    up_low = (hidden_grad * gate_pre * sigmoid).astype(low)
    second_halves = core_halves(second_low, groups)
    gate_grad = sum_gradient(second_halves, gate_low, ("x", "y"))
    up_grad = sum_gradient(second_halves, up_low, ("y", "x"))
    second_in_grad = matmul_back(gate_low, gate_full) + matmul_back(up_low, up_full)
    second_gain_grad = jnp.sum(second_in_grad * normed_two, axis=0, keepdims=True)
    middle_grad = upstream + norm_back(second_in_grad, gain_two, normed_two, scale_two)
    middle_low = middle_grad.astype(low)
    out_grad = sum_gradient(core_halves(attended, groups), middle_low, ("x", "y"))
    attended_grad = matmul_back(middle_low, out_full).astype(low)
    factor_low = jnp.concatenate(
        [
            piece[1](attended_grad[j * row_count : (j + 1) * row_count])
            for j, piece in enumerate(pieces)
        ],
        axis=0,
    )
    factor_low = jnp.pad(factor_low, ((0, 0), (0, padded - factor_count)))
    first_in_grad = matmul_back(factor_low, factor_full)
    first_gain_grad = jnp.sum(first_in_grad * normed_one, axis=0, keepdims=True)
    input_grad = (
        middle_grad + norm_back(first_in_grad, gain_one, normed_one, scale_one)
    ).astype(low)
    home_grad = give_back(input_grad, batches)
    gain_rows = jnp.concatenate([first_gain_grad, second_gain_grad], axis=0)
    left = jnp.concatenate([first_low, jnp.pad(gain_rows, ((0, 14), (0, 0))).astype(low)], axis=0)
    right = jnp.concatenate([factor_low, jnp.pad(chosen, ((0, 8), (0, 0)))], axis=0)
    factor_sum = sum_gradient(core_halves(left, groups), right, ("x", "y"))
    gain_sums = matmul_back(chosen, factor_sum.astype(low))
    return (
        home_output,
        home_grad,
        factor_sum[:, :factor_count],
        out_grad,
        gate_grad,
        up_grad,
        down_grad,
        gain_sums[0],
        gain_sums[1],
    )


def solution(mesh):
    in_specs = (
        P("rep", "shard", None),
        P("rep", "shard", None),
        P("rep", None),
        P("shard", None),
        P("shard", None),
        P("shard", None),
        P("shard", None),
        P("shard", None),
        P("shard"),
        P("shard"),
    )
    out_specs = (
        P("rep", "shard", None),
        P("rep", "shard", None),
        P("shard", None),
        P("shard", None),
        P("shard", None),
        P("shard", None),
        P("shard", None),
        P("shard"),
        P("shard"),
    )
    return jax.shard_map(
        on_device, mesh=mesh, in_specs=in_specs, out_specs=out_specs, check_vma=False
    )
```

```python
import math

import jax
import jax.numpy as jnp
from jax import lax
from jax.experimental import pallas as pl
from jax.experimental.pallas import tpu as pltpu
from jax.sharding import PartitionSpec as P

H = 16
DH = 64
RQ = 6
RK = 2


EPSILON = 1e-06


AXES = {"x": (2, 1), "y": (4, 2), "c": (1, 4)}
PIECES = 8


def bit_of(axis):
    return (lax.axis_index("rep") // AXES[axis][0]) % 2


def swap(value, axis):
    step = AXES[axis][0]
    return lax.ppermute(value, "rep", [(i, i ^ step) for i in range(lax.axis_size("rep"))])


def onward(value):
    count = lax.axis_size("shard")
    return lax.ppermute(value, "shard", [(i, (i + 1) % count) for i in range(count)])


def piece_rows(rows, by_columns):
    return rows // (PIECES // 2) if by_columns else rows // PIECES


def own_piece(shard, by_columns):
    rows, columns = shard.shape
    quarter = bit_of("y") * 2 + bit_of("x")
    core = bit_of("c")
    size = piece_rows(rows, by_columns)
    if by_columns:
        return lax.dynamic_slice(shard, (quarter * size, core * (columns // 2)), (size, columns // 2))
    return lax.dynamic_slice(shard, ((core * 4 + quarter) * size, 0), (size, columns))


def assemble(shard, parts, by_columns):
    count = lax.axis_size("shard")
    rows, columns = shard.shape
    size, width = parts[0][1].shape[2:]
    where = lax.axis_index("shard")
    mine = bit_of("c") * 4 + bit_of("y") * 2 + bit_of("x")
    masks = [mask for group, _ in parts for mask in group]
    if size % 8 or rows % 8:
        stacked = jnp.concatenate([array for _, array in parts], axis=0)
        place = jnp.zeros((PIECES,), jnp.int32).at[jnp.array(masks)].set(jnp.arange(PIECES))
        ordered = jnp.take(stacked, place[mine ^ jnp.arange(PIECES)], axis=0)
        ordered = ordered[:, (where - jnp.arange(count) - 1) % count % (count - 1)]
        if by_columns:
            ordered = ordered.reshape(2, 4, count, size, width).transpose(2, 1, 3, 0, 4)
        else:
            ordered = ordered.reshape(PIECES, count, size, width).transpose(1, 0, 2, 3)
        ordered = ordered.reshape(count, rows, columns)
        own = (jnp.arange(count) == where)[:, None, None]
        return jnp.where(own, shard[None], ordered).reshape(count * rows, columns)

    def kernel(place_ref, shard_ref, *refs):
        part_refs, out_ref, sems = refs[: len(parts)], refs[len(parts)], refs[len(parts) + 1]
        here, piece = place_ref[0], place_ref[1]
        copies = [
            pltpu.make_async_copy(
                shard_ref, out_ref.at[pl.ds(pl.multiple_of(here * rows, 8), rows), :], sems.at[0]
            )
        ]
        for (group, _), ref in zip(parts, part_refs):
            for slot, mask in enumerate(group):
                target = piece ^ mask
                for step in range(1, count):
                    source = lax.rem(here - step + count, count)
                    if by_columns:
                        row = source * rows + lax.rem(target, 4) * size
                        column = pl.ds(pl.multiple_of((target // 4) * width, 128), width)
                    else:
                        row = source * rows + target * size
                        column = slice(None)
                    copies.append(
                        pltpu.make_async_copy(
                            ref.at[slot, step - 1],
                            out_ref.at[pl.ds(pl.multiple_of(row, 8), size), column],
                            sems.at[len(copies)],
                        )
                    )
        for copy in copies:
            copy.start()
        for copy in copies:
            copy.wait()

    total = 1 + PIECES * (count - 1)
    return pl.pallas_call(
        kernel,
        out_shape=jax.ShapeDtypeStruct((count * rows, columns), shard.dtype),
        in_specs=[pl.BlockSpec(memory_space=pltpu.SMEM)]
        + [pl.BlockSpec(memory_space=pl.ANY)] * (1 + len(parts)),
        out_specs=pl.BlockSpec(memory_space=pltpu.VMEM),
        scratch_shapes=[pltpu.SemaphoreType.DMA((total,))],
        name="assemble",
        cost_estimate=pl.CostEstimate(
            flops=0, transcendentals=0, bytes_accessed=2 * 2 * count * rows * columns
        ),
    )(jnp.stack([where, mine]).astype(jnp.int32), shard, *[array for _, array in parts])


def gather_weight(shard, order, by_columns=False):
    first, second = order
    piece = own_piece(shard, by_columns)
    ring = []
    for _ in range(lax.axis_size("shard") - 1):
        piece = onward(piece)
        ring.append(piece)
    ring = jnp.stack(ring)
    one = jnp.stack([ring, swap(ring, first)])
    two = swap(one, second)
    a, b, c = AXES[first][1], AXES[second][1], AXES["c"][1]
    parts = (
        ((0, a), one),
        ((b, a | b), two),
        ((c, c | a), swap(one, "c")),
        ((c | b, c | a | b), swap(two, "c")),
    )
    return assemble(shard, parts, by_columns)


def pick(value, index, axis):
    return lax.dynamic_index_in_dim(value, index, axis, keepdims=False)


def core_halves(value, blocks, axis=1):
    width = value.shape[axis] // blocks // 2

    def half(start):
        cut = [lax.slice_in_dim(value, (2 * j + start) * width, (2 * j + start + 1) * width, axis=axis) for j in range(blocks)]
        return jnp.concatenate(cut, axis=axis)

    low, high = half(0), half(1)
    second = bit_of("c") == 1
    return jnp.where(second, high, low), jnp.where(second, low, high)


def sum_gradient(left, right, order, by_columns=False, axis=0, right_axis=0):
    count = lax.axis_size("shard")
    low = jnp.bfloat16

    def outer(left, right):
        return contract(left, right, (axis, right_axis))

    if by_columns:
        keep, send = outer(left, right[0]), outer(left, right[1])
    else:
        keep, send = outer(left[0], right), outer(left[1], right)
    got = swap(send.astype(low), "c")
    total = (keep + got.astype(jnp.float32)).astype(low)
    rows, width = total.shape
    size = rows // count // 4
    total = total.reshape(count, 2, 2, size, width)
    dims = {"y": 1, "x": 2}
    first, second = order
    for axis, dim in ((first, dims[first]), (second, 1)):
        other = pick(total, 1 - bit_of(axis), dim)
        got = swap(other, axis)
        total = (pick(total, bit_of(axis), dim).astype(jnp.float32) + got.astype(jnp.float32)).astype(low)
    here = lax.axis_index("shard")
    part = pick(total, (here - 1) % count, 0)
    for step in range(1, count):
        part = onward(part)
        mine = pick(total, (here - 1 - step) % count, 0)
        part = (part.astype(jnp.float32) + mine.astype(jnp.float32)).astype(low)
    extra = lax.axis_size("rep") // PIECES
    if extra > 1:
        groups = [[i + PIECES * j for j in range(extra)] for i in range(PIECES)]
        part = lax.psum(part, "rep", axis_index_groups=groups)

    def both(value, axis, dim):
        got = swap(value, axis)
        second_half = bit_of(axis) == 1
        return jnp.stack(
            [jnp.where(second_half, got, value), jnp.where(second_half, value, got)], axis=dim
        )

    quarters = both(part, first, 0)
    quarters = both(quarters, second, 0 if second == "y" else 1)
    quarters = quarters.reshape(4 * size, width)
    whole = both(quarters, "c", 1 if by_columns else 0)
    whole = whole.reshape(4 * size, 2 * width) if by_columns else whole.reshape(8 * size, width)
    return whole.astype(jnp.float32)


def turned(ref, start, cosine, sine_part, direction):
    half = DH // 2
    top, bottom = ref[start : start + half, :], ref[start + half : start + DH, :]
    return (
        top * cosine - direction * bottom * sine_part,
        bottom * cosine + direction * top * sine_part,
    )


FACTOR_ROWS = {"aq": 0, "ak": RQ * H, "av": (RQ + RK) * H, "bq": (RQ + 2 * RK) * H}
FACTOR_ROWS["bk"] = FACTOR_ROWS["bq"] + RQ * DH
FACTOR_ROWS["bv"] = FACTOR_ROWS["bk"] + RK * DH
SCORE_SCALE = DH**-0.5
LOG2E = math.log2(math.e)


def turn_all(factors_ref, cosine, sine_part, turned_ref):
    for slot in range(RQ + RK):
        top, bottom = turned(factors_ref, FACTOR_ROWS["bq"] + slot * DH, cosine, sine_part, 1.0)
        turned_ref[slot * DH : slot * DH + DH // 2, :] = top
        turned_ref[slot * DH + DH // 2 : (slot + 1) * DH, :] = bottom


def score_mask(length, rows):
    keys = lax.broadcasted_iota(jnp.int32, (rows, rows), 0)
    queries = lax.broadcasted_iota(jnp.int32, (rows, rows), 1)
    return jnp.where((keys <= queries) & (keys < length), 0.0, -1e30)


def contract(left, right, dims):
    return lax.dot_general(left, right, ((dims[:1], dims[1:]), ((), ())), preferred_element_type=jnp.float32)


def forward_kernel(
    length_ref, factors_ref, cosine_ref, sine_ref, out_ref, q_ref, k_ref, v_ref, lse_ref, turned_ref, mask_ref
):
    rows = factors_ref.shape[1]
    turn_all(factors_ref, cosine_ref[...], sine_ref[...], turned_ref)
    mask_ref[...] = score_mask(length_ref[pl.program_id(0)], rows)

    def mix(head, weight_row, base_ref, base_row, rank):
        total = None
        for r in range(rank):
            weight = factors_ref[pl.ds(weight_row + r * H + head, 1), :]
            term = weight * base_ref[base_row + r * DH : base_row + (r + 1) * DH, :]
            total = term if total is None else total + term
        return (total * (1.0 / rank)).astype(jnp.bfloat16)

    def one_head(head):
        span = pl.ds(pl.multiple_of(head * DH, DH), DH)
        query = mix(head, FACTOR_ROWS["aq"], turned_ref, 0, RQ)
        key = mix(head, FACTOR_ROWS["ak"], turned_ref, RQ * DH, RK)
        value = mix(head, FACTOR_ROWS["av"], factors_ref, FACTOR_ROWS["bv"], RK)
        q_ref[span, :] = query
        k_ref[span, :] = key
        v_ref[span, :] = value
        scores = contract(key, query, (0, 0)) + mask_ref[...]
        top = jnp.max(scores, axis=0, keepdims=True)
        shifted = jnp.exp2((scores - top) * (SCORE_SCALE * LOG2E))
        total = jnp.sum(shifted, axis=0, keepdims=True)
        lse_ref[pl.ds(head, 1), :] = top * SCORE_SCALE + jnp.log(total)
        probs = (shifted * (1.0 / total)).astype(jnp.bfloat16)
        out_ref[span, :] = contract(value, probs, (1, 0)).astype(jnp.bfloat16)

    @pl.loop(0, H // HEADS_AT_ONCE)
    def _(step):
        for j in range(HEADS_AT_ONCE):
            one_head(step * HEADS_AT_ONCE + j)


def backward_kernel(
    length_ref, factors_ref, cosine_ref, sine_ref, q_ref, k_ref, v_ref, lse_ref, grad_ref,
    out_ref, turned_ref, mask_ref, sums_ref, heads_ref,
):
    rows = factors_ref.shape[1]
    turn_all(factors_ref, cosine_ref[...], sine_ref[...], turned_ref)
    mask_ref[...] = score_mask(length_ref[pl.program_id(0)], rows)
    sums_ref[...] = jnp.zeros_like(sums_ref)

    def unmix(head, grad, weight_row, base_ref, base_row, sum_row, rank):
        for r in range(rank):
            weight = factors_ref[pl.ds(weight_row + r * H + head, 1), :]
            base = base_ref[base_row + r * DH : base_row + (r + 1) * DH, :]
            heads_ref[pl.ds(weight_row + r * H + head, 1), :] = jnp.sum(grad * base, axis=0, keepdims=True)
            sums_ref[sum_row + r * DH : sum_row + (r + 1) * DH, :] += grad * weight

    def one_head(head):
        span = pl.ds(pl.multiple_of(head * DH, DH), DH)
        query, key, value, grad = q_ref[span, :], k_ref[span, :], v_ref[span, :], grad_ref[span, :]
        scores = contract(key, query, (0, 0)) + mask_ref[...]
        lse = lse_ref[pl.ds(head, 1), :] * LOG2E
        probs = jnp.exp2(scores * (SCORE_SCALE * LOG2E) - lse)
        prob_grad = contract(value, grad, (0, 0))
        delta = jnp.sum(probs * prob_grad, axis=0, keepdims=True)
        score_grad = (probs * (prob_grad - delta)).astype(jnp.bfloat16)
        query_grad = contract(key, score_grad, (1, 0)) * (SCORE_SCALE / RQ)
        key_grad = contract(query, score_grad, (1, 1)) * (SCORE_SCALE / RK)
        value_grad = contract(grad, probs.astype(jnp.bfloat16), (1, 1)) * (1.0 / RK)
        unmix(head, query_grad, FACTOR_ROWS["aq"], turned_ref, 0, 0, RQ)
        unmix(head, key_grad, FACTOR_ROWS["ak"], turned_ref, RQ * DH, RQ * DH, RK)
        unmix(head, value_grad, FACTOR_ROWS["av"], factors_ref, FACTOR_ROWS["bv"], (RQ + RK) * DH, RK)

    @pl.loop(0, H // HEADS_AT_ONCE)
    def _(step):
        for j in range(HEADS_AT_ONCE):
            one_head(step * HEADS_AT_ONCE + j)

    low = jnp.bfloat16
    start = FACTOR_ROWS["bq"]
    out_ref[0:start, :] = heads_ref[...].astype(low)
    for slot in range(RQ + RK):
        top, bottom = turned(sums_ref, slot * DH, cosine_ref[...], sine_ref[...], -1.0)
        row = start + slot * DH
        out_ref[row : row + DH // 2, :] = top.astype(low)
        out_ref[row + DH // 2 : row + DH, :] = bottom.astype(low)
    row = FACTOR_ROWS["bv"]
    out_ref[row : row + RK * DH, :] = sums_ref[(RQ + RK) * DH :, :].astype(low)
    rest = out_ref.shape[0] - row - RK * DH
    out_ref[row + RK * DH :, :] = jnp.zeros((rest, rows), low)


HEADS_AT_ONCE = 2


def rotary_columns(seq_length):
    position = lax.iota(jnp.float32, seq_length)
    freq = jnp.exp(lax.iota(jnp.float32, DH // 2) * (-2.0 * math.log(10000.0) / DH))
    angle = freq[:, None] * position[None, :]
    return jnp.cos(angle), jnp.sin(angle)


def per_sequence(height, length):
    return pl.BlockSpec((height, length), lambda j: (0, j))


def attend(factors, lengths, tables):
    batches = lengths.shape[0]
    height, positions = factors.shape
    rows = positions // batches
    width = H * DH
    whole = pl.BlockSpec((DH // 2, rows), lambda j: (0, 0))
    flops = batches * H * rows * rows * DH * 2
    results = pl.pallas_call(
        forward_kernel,
        grid=(batches,),
        out_shape=[jax.ShapeDtypeStruct((width, positions), jnp.bfloat16)] * 4
        + [jax.ShapeDtypeStruct((H, positions), jnp.float32)],
        in_specs=[pl.BlockSpec(memory_space=pltpu.SMEM), per_sequence(height, rows), whole, whole],
        out_specs=[per_sequence(width, rows)] * 4 + [per_sequence(H, rows)],
        scratch_shapes=[
            pltpu.VMEM(((RQ + RK) * DH, rows), jnp.float32),
            pltpu.VMEM((rows, rows), jnp.float32),
        ],
        name="attend",
        cost_estimate=pl.CostEstimate(
            flops=8 * flops, transcendentals=0, bytes_accessed=4 * height * positions + 8 * width * positions
        ),
    )(lengths, factors, *tables)
    return results[0], tuple(results[1:])


def attend_back(factors, lengths, tables, kept, grad):
    batches = lengths.shape[0]
    height, positions = factors.shape
    rows = positions // batches
    width = H * DH
    whole = pl.BlockSpec((DH // 2, rows), lambda j: (0, 0))
    flops = batches * H * rows * rows * DH * 2
    return pl.pallas_call(
        backward_kernel,
        grid=(batches,),
        out_shape=jax.ShapeDtypeStruct((height, positions), jnp.bfloat16),
        in_specs=[pl.BlockSpec(memory_space=pltpu.SMEM), per_sequence(height, rows), whole, whole]
        + [per_sequence(width, rows)] * 3
        + [per_sequence(H, rows), per_sequence(width, rows)],
        out_specs=per_sequence(height, rows),
        scratch_shapes=[
            pltpu.VMEM(((RQ + RK) * DH, rows), jnp.float32),
            pltpu.VMEM((rows, rows), jnp.float32),
            pltpu.VMEM(((RQ + 2 * RK) * DH, rows), jnp.float32),
            pltpu.VMEM(((RQ + 2 * RK) * H, rows), jnp.float32),
        ],
        name="attend_back",
        cost_estimate=pl.CostEstimate(
            flops=20 * flops, transcendentals=0, bytes_accessed=6 * height * positions + 8 * width * positions
        ),
    )(lengths, factors, *tables, *kept, grad)


def matmul(left, right):
    return contract(left, right, (1, 0))


def matmul_back(left, right):
    return contract(left, right, (1, 1))


def norm_scale(value):
    return lax.rsqrt(jnp.mean(value * value, axis=-1, keepdims=True) + EPSILON)


def norm_back(grad, gain, normed, scale):
    scaled = grad * gain
    return scale * (scaled - normed * jnp.mean(scaled * normed, axis=-1, keepdims=True))


def deal(value):
    groups = lax.axis_size("shard")
    batches = value.shape[0] // groups
    rows, width = value.shape[1:]
    dealt = lax.all_to_all(
        value.reshape(batches, groups, rows, width), "shard", split_axis=1, concat_axis=2, tiled=True
    )
    return dealt.reshape(batches * groups * rows, width)


def give_back(value, batches):
    groups = lax.axis_size("shard")
    width = value.shape[-1]
    home = lax.all_to_all(
        value.reshape(batches, 1, -1, width), "shard", split_axis=2, concat_axis=1, tiled=True
    )
    return home.reshape(batches * groups, -1, width)


def on_device(
    tokens,
    cotangent,
    lengths,
    factor_weight,
    out_weight,
    gate_weight,
    up_weight,
    down_weight,
    first_gain,
    second_gain,
):
    low = jnp.bfloat16
    groups = lax.axis_size("shard")
    batches = tokens.shape[0] // groups
    row_count = tokens.shape[1] * groups
    factor_count = factor_weight.shape[1]
    padded = -(-(factor_count + 2) // 128) * 128
    own_slot = lax.iota(jnp.int32, groups) == lax.axis_index("shard")
    own_lengths = jnp.sum(jnp.where(own_slot[None, :], lengths.reshape(batches, groups), 0), axis=1)
    live = (lax.iota(jnp.int32, row_count)[None, :] < own_lengths[:, None]).reshape(-1, 1)

    inputs = deal(tokens).astype(jnp.float32)
    shard = jnp.concatenate([factor_weight, first_gain[:, None], second_gain[:, None]], axis=1)
    shard = jnp.pad(shard, ((0, 0), (0, padded - factor_count - 2)))
    factor_full = gather_weight(shard, ("x", "y"))
    out_full = gather_weight(out_weight, ("x", "y"))
    gate_full = gather_weight(gate_weight, ("x", "y"))
    up_full = gather_weight(up_weight, ("y", "x"))
    down_full = gather_weight(down_weight, ("y", "x"), by_columns=True)
    upstream = jnp.where(live, deal(cotangent).astype(jnp.float32), 0.0)
    upstream_low = upstream.astype(low)

    at = lax.broadcasted_iota(jnp.int32, (8, padded), 1) - factor_count
    chosen = (at == lax.broadcasted_iota(jnp.int32, (8, padded), 0)).astype(low)
    gains = matmul_back(chosen, factor_full)
    gain_one, gain_two = gains[0:1], gains[1:2]

    scale_one = norm_scale(inputs)
    normed_one = inputs * scale_one
    first_low = (normed_one * gain_one).astype(low)
    factors = contract(factor_full, first_low, (0, 1))
    tables = rotary_columns(row_count)
    attended, kept = attend(factors, own_lengths, tables)
    middle = inputs + contract(attended, out_full, (0, 0))
    scale_two = norm_scale(middle)
    normed_two = middle * scale_two
    second_low = (normed_two * gain_two).astype(low)
    gate_pre = matmul(second_low, gate_full)
    up_pre = matmul(second_low, up_full)
    sigmoid = jax.nn.sigmoid(gate_pre)
    hidden = (gate_pre * sigmoid * up_pre).astype(low)
    result = middle + matmul(hidden, down_full)
    output = jnp.where(live, result, 0.0).astype(low)
    home_output = give_back(output, batches)

    down_grad = sum_gradient(hidden, core_halves(upstream_low, 1), ("y", "x"), by_columns=True)
    hidden_grad = matmul_back(upstream_low, down_full)
    gate_low = (hidden_grad * up_pre * sigmoid * (1.0 + gate_pre * (1.0 - sigmoid))).astype(low)
    up_low = (hidden_grad * gate_pre * sigmoid).astype(low)
    second_halves = core_halves(second_low, groups)
    gate_grad = sum_gradient(second_halves, gate_low, ("x", "y"))
    up_grad = sum_gradient(second_halves, up_low, ("y", "x"))
    second_in_grad = matmul_back(gate_low, gate_full) + matmul_back(up_low, up_full)
    second_gain_grad = jnp.sum(second_in_grad * normed_two, axis=0, keepdims=True)
    middle_grad = upstream + norm_back(second_in_grad, gain_two, normed_two, scale_two)
    middle_low = middle_grad.astype(low)
    out_grad = sum_gradient(core_halves(attended, groups, 0), middle_low, ("x", "y"), axis=1)
    attended_grad = matmul_back(out_full, middle_low).astype(low)
    factor_low = attend_back(factors, own_lengths, tables, kept, attended_grad)
    first_in_grad = contract(factor_low, factor_full, (0, 1))
    first_gain_grad = jnp.sum(first_in_grad * normed_one, axis=0, keepdims=True)
    input_grad = (
        middle_grad + norm_back(first_in_grad, gain_one, normed_one, scale_one)
    ).astype(low)
    home_grad = give_back(input_grad, batches)
    gain_rows = jnp.concatenate([first_gain_grad, second_gain_grad], axis=0)
    left = jnp.concatenate([first_low, jnp.pad(gain_rows, ((0, 126), (0, 0))).astype(low)], axis=0)
    right = jnp.concatenate([factor_low, jnp.pad(chosen.T, ((0, 0), (0, 120)))], axis=1)
    factor_sum = sum_gradient(core_halves(left, groups), right, ("x", "y"), right_axis=1)
    gain_sums = matmul_back(chosen, factor_sum.astype(low))
    return (
        home_output,
        home_grad,
        factor_sum[:, :factor_count],
        out_grad,
        gate_grad,
        up_grad,
        down_grad,
        gain_sums[0],
        gain_sums[1],
    )


def solution(mesh):
    in_specs = (
        P("rep", "shard", None),
        P("rep", "shard", None),
        P("rep", None),
        P("shard", None),
        P("shard", None),
        P("shard", None),
        P("shard", None),
        P("shard", None),
        P("shard"),
        P("shard"),
    )
    out_specs = (
        P("rep", "shard", None),
        P("rep", "shard", None),
        P("shard", None),
        P("shard", None),
        P("shard", None),
        P("shard", None),
        P("shard", None),
        P("shard"),
        P("shard"),
    )
    return jax.shard_map(
        on_device, mesh=mesh, in_specs=in_specs, out_specs=out_specs, check_vma=False
    )
```

```python
import math

import jax
import jax.numpy as jnp
from jax import lax
from jax.experimental import pallas as pl
from jax.experimental.pallas import tpu as pltpu
from jax.sharding import PartitionSpec as P

H = 16
DH = 64
RQ = 6
RK = 2


EPSILON = 1e-06


AXES = {"x": (2, 1), "y": (4, 2), "c": (1, 4)}
PIECES = 8


def bit_of(axis):
    return (lax.axis_index("rep") // AXES[axis][0]) % 2


def swap(value, axes):
    step = sum(AXES[axis][0] for axis in axes)
    return lax.ppermute(value, "rep", [(i, i ^ step) for i in range(lax.axis_size("rep"))])


def onward(value, distance):
    count = lax.axis_size("shard")
    return lax.ppermute(value, "shard", [(i, (i + distance) % count) for i in range(count)])


def after(value, *tokens):
    return lax.optimization_barrier((value, *tokens))[0]


def own_piece(shard, by_columns=False):
    rows, columns = shard.shape
    quarter = bit_of("y") * 2 + bit_of("x")
    core = bit_of("c")
    if by_columns:
        size = rows // (PIECES // 2)
        return lax.dynamic_slice(shard, (quarter * size, core * (columns // 2)), (size, columns // 2))
    size = rows // PIECES
    return lax.dynamic_slice(shard, ((core * 4 + quarter) * size, 0), (size, columns))


def assemble(shards, parts, by_columns=False):
    count = lax.axis_size("shard")
    width = parts[0][1].shape[3]
    sizes = [shard.shape[0] // (PIECES // 2 if by_columns else PIECES) for shard in shards]
    where = lax.axis_index("shard")
    mine = bit_of("c") * 4 + bit_of("y") * 2 + bit_of("x")
    outs = [jax.ShapeDtypeStruct((count * shard.shape[0], shard.shape[1]), shard.dtype) for shard in shards]
    if any(size % 8 for size in sizes):
        masks = [mask for group, _ in parts for mask in group]
        stacked = jnp.concatenate([array for _, array in parts], axis=0)
        place = jnp.array([masks.index(mask) for mask in range(PIECES)], jnp.int32)
        ordered = jnp.take(stacked, place[mine ^ jnp.arange(PIECES)], axis=0)
        ordered = ordered[:, (where - jnp.arange(count) - 1) % count % (count - 1)]
        own = (jnp.arange(count) == where)[:, None, None]
        results, start = [], 0
        for shard, size in zip(shards, sizes):
            block = ordered[:, :, start : start + size]
            start += size
            if by_columns:
                block = block.reshape(2, 4, count, size, width).transpose(2, 1, 3, 0, 4)
            else:
                block = block.transpose(1, 0, 2, 3)
            block = block.reshape((count,) + shard.shape)
            results.append(jnp.where(own, shard[None], block).reshape(-1, shard.shape[1]))
        return results

    def kernel(place_ref, *refs):
        many = len(shards)
        shard_refs, part_refs = refs[:many], refs[many : many + len(parts)]
        out_refs, whole_refs = refs[many + len(parts) : 2 * many + len(parts)], refs[2 * many + len(parts) : -2]
        sems, out_sems = refs[-2:]
        here, piece = place_ref[0], place_ref[1]
        rows = [shard.shape[0] for shard in shards]

        def block(ref, source, i):
            return ref.at[pl.ds(pl.multiple_of(source * rows[i], 8), rows[i]), :]

        arrivals, issued = [], 0
        for step in range(count):
            source = lax.rem(here - step + count, count)
            copies = []
            if step == 0:
                for i, whole_ref in enumerate(whole_refs):
                    copies.append((shard_refs[i], block(whole_ref, source, i)))
            else:
                for (group, _), part_ref in zip(parts, part_refs):
                    for slot, mask in enumerate(group):
                        target = piece ^ mask
                        start = 0
                        for i, (size, whole_ref) in enumerate(zip(sizes, whole_refs)):
                            if by_columns:
                                row = lax.rem(target, 4) * size
                                column = pl.ds(pl.multiple_of((target // 4) * width, 128), width)
                            else:
                                row, column = target * size, slice(None)
                            row = pl.multiple_of(source * rows[i] + row, 8)
                            copies.append(
                                (
                                    part_ref.at[slot, step - 1, start : start + size, :],
                                    whole_ref.at[pl.ds(row, size), column],
                                )
                            )
                            start += size
            made = []
            for origin, goal in copies:
                made.append(pltpu.make_async_copy(origin, goal, sems.at[issued]))
                made[-1].start()
                issued += 1
            arrivals.append((source, made))
        leaving = []
        for step, (source, made) in enumerate(arrivals):
            for copy in made:
                copy.wait()
            for i in range(many):
                leaving.append(
                    pltpu.make_async_copy(
                        block(whole_refs[i], source, i), block(out_refs[i], source, i), out_sems.at[step * many + i]
                    )
                )
                leaving[-1].start()
        for copy in leaving:
            copy.wait()

    total = sum(out.shape[0] * out.shape[1] * 2 for out in outs)
    return pl.pallas_call(
        kernel,
        out_shape=outs,
        in_specs=[pl.BlockSpec(memory_space=pltpu.SMEM)]
        + [pl.BlockSpec(memory_space=pl.ANY)] * (len(shards) + len(parts)),
        out_specs=[pl.BlockSpec(memory_space=pl.ANY)] * len(shards),
        scratch_shapes=[pltpu.VMEM(out.shape, out.dtype) for out in outs]
        + [
            pltpu.SemaphoreType.DMA((len(shards) * (1 + PIECES * (count - 1)),)),
            pltpu.SemaphoreType.DMA((len(shards) * count,)),
        ],
        name="assemble",
        cost_estimate=pl.CostEstimate(flops=0, transcendentals=0, bytes_accessed=2 * total),
    )(jnp.stack([where, mine]).astype(jnp.int32), *shards, *[array for _, array in parts])


def send_round(piece):
    sent = [onward(piece, step) for step in range(1, lax.axis_size("shard"))]
    ring = jnp.stack(sent)
    return lax.optimization_barrier(ring)


def gather_direct(ring, token=None):
    got = [swap(ring, axes) for axes in ("xy", "x", "y")]
    if token is not None:
        ring = after(ring, token)
    near = jnp.stack([ring, got[1], got[2], got[0]])
    return (((0, 1, 2, 3), near), ((4, 5, 6, 7), swap(near, "c")))


def pick(value, index, axis):
    return lax.dynamic_index_in_dim(value, index, axis, keepdims=False)


def core_halves(value, blocks, axis=1):
    width = value.shape[axis] // blocks // 2

    def half(start):
        cut = [
            lax.slice_in_dim(value, (2 * j + start) * width, (2 * j + start + 1) * width, axis=axis)
            for j in range(blocks)
        ]
        return jnp.concatenate(cut, axis=axis)

    low, high = half(0), half(1)
    second = bit_of("c") == 1
    return jnp.where(second, high, low), jnp.where(second, low, high)


def add_low(*terms):
    total = terms[0].astype(jnp.float32)
    for term in terms[1:]:
        total = total + term.astype(jnp.float32)
    return total.astype(jnp.bfloat16)


def by_quarter(total):
    count = lax.axis_size("shard")
    rows, width = total.shape
    return total.reshape(count, 2, 2, rows // count // 4, width)


def sum_near(total, order):
    first, second = order
    for axis, dim in ((first, {"y": 1, "x": 2}[first]), (second, 1)):
        other = pick(total, 1 - bit_of(axis), dim)
        got = swap(other, axis)
        total = add_low(pick(total, bit_of(axis), dim), got)
    return total


def sum_near_direct(total):
    quarter = bit_of("y") * 2 + bit_of("x")
    total = total.reshape((total.shape[0], 4) + total.shape[3:])
    got = [swap(pick(total, quarter ^ mask, 1), axes) for mask, axes in ((3, "xy"), (1, "x"), (2, "y"))]
    return add_low(pick(total, quarter, 1), *got)


def sum_far(total):
    count = lax.axis_size("shard")
    here = lax.axis_index("shard")
    got = [onward(pick(total, (here + step) % count, 0), step) for step in range(1, count)]
    part = add_low(pick(total, here, 0), *got)
    extra = lax.axis_size("rep") // PIECES
    if extra > 1:
        groups = [[i + PIECES * j for j in range(extra)] for i in range(PIECES)]
        part = lax.psum(part, "rep", axis_index_groups=groups)
    return part


def share(part, outs, write, by_columns=False):
    size, width = part.shape
    got = [swap(part, axes) for axes in ("xy", "x", "y")]
    near = jnp.stack([part, got[1], got[2], got[0]])
    far = swap(near, "c")
    mine = bit_of("c") * 4 + bit_of("y") * 2 + bit_of("x")

    def kernel(mine_ref, near_ref, far_ref, *out_refs):
        here = pl.program_id(0) == mine_ref[0] // 4

        def lay(value_ref):
            for quarter in range(4):
                write(value_ref.at[(mine_ref[0] ^ quarter) % 4], *[out_ref.at[quarter] for out_ref in out_refs])

        @pl.when(here)
        def _():
            lay(near_ref)

        @pl.when(jnp.logical_not(here))
        def _():
            lay(far_ref)

    def goal(core, mine_ref):
        return (0, 0, core) if by_columns else (core, 0, 0)

    shapes = [
        jax.ShapeDtypeStruct((4, rows, 2 * columns) if by_columns else (8, rows, columns), kind)
        for (rows, columns), kind in outs
    ]
    return pl.pallas_call(
        kernel,
        grid_spec=pltpu.PrefetchScalarGridSpec(
            num_scalar_prefetch=1,
            grid=(2,),
            in_specs=[pl.BlockSpec((4, size, width), lambda core, mine_ref: (0, 0, 0))] * 2,
            out_specs=[pl.BlockSpec((4,) + shape, goal) for shape, _ in outs],
        ),
        out_shape=shapes,
        name="share",
        cost_estimate=pl.CostEstimate(flops=0, transcendentals=0, bytes_accessed=32 * size * width),
    )(mine.astype(jnp.int32).reshape(1), near, far)


def turned(ref, start, cosine, sine_part, direction):
    half = DH // 2
    top, bottom = ref[start : start + half, :], ref[start + half : start + DH, :]
    return (
        top * cosine - direction * bottom * sine_part,
        bottom * cosine + direction * top * sine_part,
    )


FACTOR_ROWS = {"aq": 0, "ak": RQ * H, "av": (RQ + RK) * H, "bq": (RQ + 2 * RK) * H}
FACTOR_ROWS["bk"] = FACTOR_ROWS["bq"] + RQ * DH
FACTOR_ROWS["bv"] = FACTOR_ROWS["bk"] + RK * DH
SCORE_SCALE = DH**-0.5
LOG2E = math.log2(math.e)


def turn_all(factors_ref, cosine, sine_part, turned_ref):
    for slot in range(RQ + RK):
        top, bottom = turned(factors_ref, FACTOR_ROWS["bq"] + slot * DH, cosine, sine_part, 1.0)
        turned_ref[slot * DH : slot * DH + DH // 2, :] = top
        turned_ref[slot * DH + DH // 2 : (slot + 1) * DH, :] = bottom


def score_mask(length, rows):
    keys = lax.broadcasted_iota(jnp.int32, (rows, rows), 0)
    queries = lax.broadcasted_iota(jnp.int32, (rows, rows), 1)
    return jnp.where((keys <= queries) & (keys < length), 0.0, -1e30)


def contract(left, right, dims):
    return lax.dot_general(left, right, ((dims[:1], dims[1:]), ((), ())), preferred_element_type=jnp.float32)


def forward_kernel(
    length_ref, factors_ref, cosine_ref, sine_ref, out_ref, q_ref, k_ref, v_ref, lse_ref, turned_ref, mask_ref
):
    rows = factors_ref.shape[1]
    turn_all(factors_ref, cosine_ref[...], sine_ref[...], turned_ref)
    mask_ref[...] = score_mask(length_ref[pl.program_id(0)], rows)

    def mix(head, weight_row, base_ref, base_row, rank):
        total = None
        for r in range(rank):
            weight = factors_ref[pl.ds(weight_row + r * H + head, 1), :]
            term = weight * base_ref[base_row + r * DH : base_row + (r + 1) * DH, :]
            total = term if total is None else total + term
        return (total * (1.0 / rank)).astype(jnp.bfloat16)

    def one_head(head):
        span = pl.ds(pl.multiple_of(head * DH, DH), DH)
        query = mix(head, FACTOR_ROWS["aq"], turned_ref, 0, RQ)
        key = mix(head, FACTOR_ROWS["ak"], turned_ref, RQ * DH, RK)
        value = mix(head, FACTOR_ROWS["av"], factors_ref, FACTOR_ROWS["bv"], RK)
        q_ref[span, :] = query
        k_ref[span, :] = key
        v_ref[span, :] = value
        scores = contract(key, query, (0, 0)) + mask_ref[...]
        top = jnp.max(scores, axis=0, keepdims=True)
        shifted = jnp.exp2((scores - top) * (SCORE_SCALE * LOG2E))
        total = jnp.sum(shifted, axis=0, keepdims=True)
        lse_ref[pl.ds(head, 1), :] = top * SCORE_SCALE + jnp.log(total)
        probs = (shifted * (1.0 / total)).astype(jnp.bfloat16)
        out_ref[span, :] = contract(value, probs, (1, 0)).astype(jnp.bfloat16)

    @pl.loop(0, H // HEADS_AT_ONCE)
    def _(step):
        for j in range(HEADS_AT_ONCE):
            one_head(step * HEADS_AT_ONCE + j)


def backward_kernel(
    length_ref, factors_ref, cosine_ref, sine_ref, q_ref, k_ref, v_ref, lse_ref, grad_ref,
    out_ref, turned_ref, mask_ref, sums_ref, heads_ref,
):
    rows = factors_ref.shape[1]
    turn_all(factors_ref, cosine_ref[...], sine_ref[...], turned_ref)
    mask_ref[...] = score_mask(length_ref[pl.program_id(0)], rows)
    sums_ref[...] = jnp.zeros_like(sums_ref)

    def unmix(head, grad, weight_row, base_ref, base_row, sum_row, rank):
        for r in range(rank):
            weight = factors_ref[pl.ds(weight_row + r * H + head, 1), :]
            base = base_ref[base_row + r * DH : base_row + (r + 1) * DH, :]
            heads_ref[pl.ds(weight_row + r * H + head, 1), :] = jnp.sum(grad * base, axis=0, keepdims=True)
            sums_ref[sum_row + r * DH : sum_row + (r + 1) * DH, :] += grad * weight

    def one_head(head):
        span = pl.ds(pl.multiple_of(head * DH, DH), DH)
        query, key, value, grad = q_ref[span, :], k_ref[span, :], v_ref[span, :], grad_ref[span, :]
        scores = contract(key, query, (0, 0)) + mask_ref[...]
        lse = lse_ref[pl.ds(head, 1), :] * LOG2E
        probs = jnp.exp2(scores * (SCORE_SCALE * LOG2E) - lse)
        prob_grad = contract(value, grad, (0, 0))
        delta = jnp.sum(probs * prob_grad, axis=0, keepdims=True)
        score_grad = (probs * (prob_grad - delta)).astype(jnp.bfloat16)
        query_grad = contract(key, score_grad, (1, 0)) * (SCORE_SCALE / RQ)
        key_grad = contract(query, score_grad, (1, 1)) * (SCORE_SCALE / RK)
        value_grad = contract(grad, probs.astype(jnp.bfloat16), (1, 1)) * (1.0 / RK)
        unmix(head, query_grad, FACTOR_ROWS["aq"], turned_ref, 0, 0, RQ)
        unmix(head, key_grad, FACTOR_ROWS["ak"], turned_ref, RQ * DH, RQ * DH, RK)
        unmix(head, value_grad, FACTOR_ROWS["av"], factors_ref, FACTOR_ROWS["bv"], (RQ + RK) * DH, RK)

    @pl.loop(0, H // HEADS_AT_ONCE)
    def _(step):
        for j in range(HEADS_AT_ONCE):
            one_head(step * HEADS_AT_ONCE + j)

    low = jnp.bfloat16
    start = FACTOR_ROWS["bq"]
    out_ref[0:start, :] = heads_ref[...].astype(low)
    for slot in range(RQ + RK):
        top, bottom = turned(sums_ref, slot * DH, cosine_ref[...], sine_ref[...], -1.0)
        row = start + slot * DH
        out_ref[row : row + DH // 2, :] = top.astype(low)
        out_ref[row + DH // 2 : row + DH, :] = bottom.astype(low)
    row = FACTOR_ROWS["bv"]
    out_ref[row : row + RK * DH, :] = sums_ref[(RQ + RK) * DH :, :].astype(low)
    rest = out_ref.shape[0] - row - RK * DH
    out_ref[row + RK * DH :, :] = jnp.zeros((rest, rows), low)


HEADS_AT_ONCE = 2


def rotary_columns(seq_length):
    position = lax.iota(jnp.float32, seq_length)
    freq = jnp.exp(lax.iota(jnp.float32, DH // 2) * (-2.0 * math.log(10000.0) / DH))
    angle = freq[:, None] * position[None, :]
    return jnp.cos(angle), jnp.sin(angle)


def per_sequence(height, length):
    return pl.BlockSpec((height, length), lambda j: (0, j))


def attend(factors, lengths, tables):
    batches = lengths.shape[0]
    height, positions = factors.shape
    rows = positions // batches
    width = H * DH
    whole = pl.BlockSpec((DH // 2, rows), lambda j: (0, 0))
    flops = batches * H * rows * rows * DH * 2
    results = pl.pallas_call(
        forward_kernel,
        grid=(batches,),
        out_shape=[jax.ShapeDtypeStruct((width, positions), jnp.bfloat16)] * 4
        + [jax.ShapeDtypeStruct((H, positions), jnp.float32)],
        in_specs=[pl.BlockSpec(memory_space=pltpu.SMEM), per_sequence(height, rows), whole, whole],
        out_specs=[per_sequence(width, rows)] * 4 + [per_sequence(H, rows)],
        scratch_shapes=[
            pltpu.VMEM(((RQ + RK) * DH, rows), jnp.float32),
            pltpu.VMEM((rows, rows), jnp.float32),
        ],
        name="attend",
        cost_estimate=pl.CostEstimate(
            flops=8 * flops, transcendentals=0, bytes_accessed=4 * height * positions + 8 * width * positions
        ),
    )(lengths, factors, *tables)
    return results[0], tuple(results[1:])


def attend_back(factors, lengths, tables, kept, grad):
    batches = lengths.shape[0]
    height, positions = factors.shape
    rows = positions // batches
    width = H * DH
    whole = pl.BlockSpec((DH // 2, rows), lambda j: (0, 0))
    flops = batches * H * rows * rows * DH * 2
    return pl.pallas_call(
        backward_kernel,
        grid=(batches,),
        out_shape=jax.ShapeDtypeStruct((height, positions), jnp.bfloat16),
        in_specs=[pl.BlockSpec(memory_space=pltpu.SMEM), per_sequence(height, rows), whole, whole]
        + [per_sequence(width, rows)] * 3
        + [per_sequence(H, rows), per_sequence(width, rows)],
        out_specs=per_sequence(height, rows),
        scratch_shapes=[
            pltpu.VMEM(((RQ + RK) * DH, rows), jnp.float32),
            pltpu.VMEM((rows, rows), jnp.float32),
            pltpu.VMEM(((RQ + 2 * RK) * DH, rows), jnp.float32),
            pltpu.VMEM(((RQ + 2 * RK) * H, rows), jnp.float32),
        ],
        name="attend_back",
        cost_estimate=pl.CostEstimate(
            flops=20 * flops, transcendentals=0, bytes_accessed=6 * height * positions + 8 * width * positions
        ),
    )(lengths, factors, *tables, *kept, grad)


def matmul(left, right):
    return contract(left, right, (1, 0))


def matmul_back(left, right):
    return contract(left, right, (1, 1))


def norm_scale(value):
    return lax.rsqrt(jnp.mean(value * value, axis=-1, keepdims=True) + EPSILON)


def norm_back(grad, gain, normed, scale):
    scaled = grad * gain
    return scale * (scaled - normed * jnp.mean(scaled * normed, axis=-1, keepdims=True))


def deal(value):
    groups = lax.axis_size("shard")
    batches = value.shape[0] // groups
    rows, width = value.shape[1:]
    value = value.reshape(batches, groups, rows, width).swapaxes(0, 1)
    dealt = lax.all_to_all(value, "shard", split_axis=0, concat_axis=0, tiled=True)
    return dealt.swapaxes(0, 1).reshape(batches * groups * rows, width)


def give_back(value, batches):
    groups = lax.axis_size("shard")
    width = value.shape[-1]
    value = value.reshape(batches, groups, -1, width).swapaxes(0, 1)
    home = lax.all_to_all(value, "shard", split_axis=0, concat_axis=0, tiled=True)
    return home.swapaxes(0, 1).reshape(batches * groups, -1, width)


def on_device(
    tokens,
    cotangent,
    lengths,
    factor_weight,
    out_weight,
    gate_weight,
    up_weight,
    down_weight,
    first_gain,
    second_gain,
):
    low = jnp.bfloat16
    groups = lax.axis_size("shard")
    batches = tokens.shape[0] // groups
    row_count = tokens.shape[1] * groups
    factor_count = factor_weight.shape[1]
    padded = out_weight.shape[1]
    own_slot = lax.iota(jnp.int32, groups) == lax.axis_index("shard")
    own_lengths = jnp.sum(jnp.where(own_slot[None, :], lengths.reshape(batches, groups), 0), axis=1)
    live = (lax.iota(jnp.int32, row_count)[None, :] < own_lengths[:, None]).reshape(-1, 1)

    inputs = deal(tokens).astype(jnp.float32)
    shard = jnp.concatenate([factor_weight, first_gain[:, None], second_gain[:, None]], axis=1)
    shard = jnp.pad(shard, ((0, 0), (0, padded - factor_count - 2)))
    near_ring = send_round(jnp.concatenate([own_piece(shard), own_piece(out_weight)], axis=0))
    factor_full, out_full = assemble([shard, out_weight], gather_direct(near_ring))
    gate_parts = gather_direct(send_round(own_piece(gate_weight)))
    (gate_full,) = assemble([gate_weight], gate_parts)
    up_parts = gather_direct(send_round(own_piece(up_weight)))
    (up_full,) = assemble([up_weight], up_parts)
    down_ring = send_round(own_piece(down_weight, True))
    dealt_cotangent = deal(cotangent)

    at = lax.broadcasted_iota(jnp.int32, (8, padded), 1) - factor_count
    chosen = (at == lax.broadcasted_iota(jnp.int32, (8, padded), 0)).astype(low)
    last = factor_count // 128 * 128
    gains = matmul_back(chosen[:, last : last + 128], factor_full[:, last : last + 128])
    gain_one, gain_two = gains[0:1], gains[1:2]

    scale_one = norm_scale(inputs)
    normed_one = inputs * scale_one
    first_low = (normed_one * gain_one).astype(low)
    factors = contract(factor_full, first_low, (0, 1))
    tables = rotary_columns(row_count)
    attended, kept = attend(factors, own_lengths, tables)
    middle = inputs + contract(attended, out_full, (0, 0))
    scale_two = norm_scale(middle)
    normed_two = middle * scale_two
    second_low = (normed_two * gain_two).astype(low)
    gate_pre = lax.optimization_barrier(matmul(second_low, gate_full).astype(low)).astype(jnp.float32)
    up_pre = matmul(second_low, up_full)
    sigmoid = jax.nn.sigmoid(gate_pre)
    hidden = (gate_pre * sigmoid * up_pre).astype(low)
    up_pre = lax.optimization_barrier(up_pre.astype(low)).astype(jnp.float32)

    down_parts = gather_direct(down_ring, hidden)
    (down_full,) = assemble([down_weight], down_parts, True)
    upstream = jnp.where(live, after(dealt_cotangent, hidden).astype(jnp.float32), 0.0)
    upstream_low = upstream.astype(low)
    upstream_keep, upstream_send = core_halves(upstream_low, 1)
    down_send = contract(hidden, upstream_send, (0, 0)).astype(low)
    down_got = swap(down_send, "c")
    hidden_grad = matmul_back(after(upstream_low, down_send), down_full)
    gate_low = (hidden_grad * up_pre * sigmoid * (1.0 + gate_pre * (1.0 - sigmoid))).astype(low)
    up_low = (hidden_grad * gate_pre * sigmoid).astype(low)
    down_total = by_quarter(add_low(contract(hidden, after(upstream_keep, gate_low), (0, 0)), down_got))
    second_keep, second_send = core_halves(second_low, groups)
    gate_send = contract(after(second_send, down_total), gate_low, (0, 0)).astype(low)
    gate_got = swap(gate_send, "c")
    up_send = contract(after(second_send, gate_send), up_low, (0, 0)).astype(low)
    up_got = swap(up_send, "c")
    gate_total = by_quarter(add_low(contract(after(second_keep, up_send), gate_low, (0, 0)), gate_got))
    up_total = by_quarter(add_low(contract(after(second_keep, gate_total), up_low, (0, 0)), up_got))
    gate_low, up_low = lax.optimization_barrier((gate_low, up_low, up_total))[:2]
    second_in_grad = matmul_back(gate_low, gate_full) + matmul_back(up_low, up_full)
    second_gain_grad = jnp.sum(second_in_grad * normed_two, axis=0, keepdims=True)
    middle_grad = upstream + norm_back(second_in_grad, gain_two, normed_two, scale_two)
    middle_low = middle_grad.astype(low)
    attended_grad = matmul_back(out_full, middle_low).astype(low)
    attended_keep, attended_send = core_halves(attended, groups, 0)
    out_send = contract(attended_send, middle_low, (1, 0)).astype(low)
    out_got = swap(out_send, "c")
    out_total = by_quarter(add_low(contract(attended_keep, middle_low, (1, 0)), out_got))
    result = middle + matmul(after(hidden, out_send), down_full)
    output = jnp.where(live, result, 0.0).astype(low)
    home_output = give_back(output, batches)
    factor_low = attend_back(factors, own_lengths, tables, kept, after(attended_grad, output, out_total))

    gate_near = sum_near(gate_total, ("x", "y"))
    up_near = sum_near(up_total, ("y", "x"))
    pair_total = jnp.concatenate([gate_near, up_near], axis=1)
    first_in_grad = contract(after(factor_low, pair_total), factor_full, (0, 1))
    first_gain_grad = jnp.sum(first_in_grad * normed_one, axis=0, keepdims=True)
    input_grad = (
        middle_grad + norm_back(first_in_grad, gain_one, normed_one, scale_one)
    ).astype(low)
    home_grad = give_back(input_grad, batches)
    gain_rows = jnp.concatenate([first_gain_grad, second_gain_grad], axis=0)
    left = jnp.concatenate([first_low, jnp.pad(gain_rows, ((0, 126), (0, 0))).astype(low)], axis=0)
    right = jnp.concatenate([factor_low, jnp.pad(chosen.T, ((0, 0), (0, 120)))], axis=1)
    left_keep, left_send = core_halves(left, groups)
    factor_send = contract(left_send, right, (0, 1)).astype(low)
    factor_got = swap(factor_send, "c")
    factor_total = by_quarter(add_low(contract(left_keep, right, (0, 1)), factor_got))

    full = jnp.float32
    down_part = sum_far(sum_near(down_total, ("y", "x")))
    pair_part = sum_far(pair_total)
    near_total = [sum_near_direct(factor_total), sum_near_direct(out_total)]
    near_part = sum_far(jnp.concatenate(near_total, axis=1))

    def widen(value_ref, out_ref):
        out_ref[...] = value_ref[...].astype(full)

    def widen_pair(value_ref, gate_ref, up_ref):
        size = gate_ref.shape[0]
        gate_ref[...] = value_ref[:size, :].astype(full)
        up_ref[...] = value_ref[size:, :].astype(full)

    def widen_near(value_ref, factor_ref, out_ref):
        size = out_ref.shape[0]
        value = value_ref[...].astype(full)
        factor_ref[...] = value[:size]
        out_ref[...] = value[size:]

    (down_grad,) = share(down_part, [(down_part.shape, full)], widen, by_columns=True)
    size = gate_weight.shape[0] // PIECES
    block = (size, gate_weight.shape[1])
    gate_grad, up_grad = share(pair_part, [(block, full)] * 2, widen_pair)
    factor_grad, out_grad = share(near_part, [((size, padded), full)] * 2, widen_near)
    factor_grad = factor_grad.reshape(-1, padded)
    gain_sums = matmul_back(chosen[:, last : last + 128], factor_grad[:, last : last + 128].astype(low))
    return (
        home_output,
        home_grad,
        factor_grad[:, :factor_count],
        out_grad.reshape(out_weight.shape),
        gate_grad.reshape(gate_weight.shape),
        up_grad.reshape(up_weight.shape),
        down_grad.reshape(down_weight.shape),
        gain_sums[0],
        gain_sums[1],
    )


def solution(mesh):
    in_specs = (
        P("rep", "shard", None),
        P("rep", "shard", None),
        P("rep", None),
        P("shard", None),
        P("shard", None),
        P("shard", None),
        P("shard", None),
        P("shard", None),
        P("shard"),
        P("shard"),
    )
    out_specs = (
        P("rep", "shard", None),
        P("rep", "shard", None),
        P("shard", None),
        P("shard", None),
        P("shard", None),
        P("shard", None),
        P("shard", None),
        P("shard"),
        P("shard"),
    )
    return jax.shard_map(on_device, mesh=mesh, in_specs=in_specs, out_specs=out_specs, check_vma=False)
```

```python
import functools
import math

import jax
import jax.numpy as jnp
from jax import lax
from jax.experimental import pallas as pl
from jax.experimental.pallas import tpu as pltpu
from jax.sharding import PartitionSpec as P

H = 16
DH = 64
RQ = 6
RK = 2


EPSILON = 1e-06


AXES = {"x": (2, 1), "y": (4, 2), "c": (1, 4)}
PIECES = 8


def bit_of(axis):
    return (lax.axis_index("rep") // AXES[axis][0]) % 2


def swap(value, axes):
    step = sum(AXES[axis][0] for axis in axes)
    return lax.ppermute(value, "rep", [(i, i ^ step) for i in range(lax.axis_size("rep"))])


def onward(value, distance):
    count = lax.axis_size("shard")
    return lax.ppermute(value, "shard", [(i, (i + distance) % count) for i in range(count)])


def after(value, *tokens):
    return lax.optimization_barrier((value, *tokens))[0]


def own_piece(shard, by_columns=False):
    rows, columns = shard.shape
    quarter = bit_of("y") * 2 + bit_of("x")
    core = bit_of("c")
    if by_columns:
        size = rows // (PIECES // 2)
        return lax.dynamic_slice(shard, (quarter * size, core * (columns // 2)), (size, columns // 2))
    size = rows // PIECES
    return lax.dynamic_slice(shard, ((core * 4 + quarter) * size, 0), (size, columns))


def assemble(shards, parts, by_columns=False):
    count = lax.axis_size("shard")
    width = parts[0][1].shape[3]
    sizes = [shard.shape[0] // (PIECES // 2 if by_columns else PIECES) for shard in shards]
    where = lax.axis_index("shard")
    mine = bit_of("c") * 4 + bit_of("y") * 2 + bit_of("x")
    outs = [jax.ShapeDtypeStruct((count * shard.shape[0], shard.shape[1]), shard.dtype) for shard in shards]
    if any(size % 8 for size in sizes):
        masks = [mask for group, _ in parts for mask in group]
        stacked = jnp.concatenate([array for _, array in parts], axis=0)
        place = jnp.array([masks.index(mask) for mask in range(PIECES)], jnp.int32)
        ordered = jnp.take(stacked, place[mine ^ jnp.arange(PIECES)], axis=0)
        ordered = ordered[:, (where - jnp.arange(count) - 1) % count % (count - 1)]
        own = (jnp.arange(count) == where)[:, None, None]
        results, start = [], 0
        for shard, size in zip(shards, sizes):
            block = ordered[:, :, start : start + size]
            start += size
            if by_columns:
                block = block.reshape(2, 4, count, size, width).transpose(2, 1, 3, 0, 4)
            else:
                block = block.transpose(1, 0, 2, 3)
            block = block.reshape((count,) + shard.shape)
            results.append(jnp.where(own, shard[None], block).reshape(-1, shard.shape[1]))
        return results

    def kernel(place_ref, *refs):
        many = len(shards)
        shard_refs, part_refs = refs[:many], refs[many : many + len(parts)]
        out_refs, whole_refs = refs[many + len(parts) : 2 * many + len(parts)], refs[2 * many + len(parts) : -2]
        sems, out_sems = refs[-2:]
        here, piece = place_ref[0], place_ref[1]
        rows = [shard.shape[0] for shard in shards]

        def block(ref, source, i):
            return ref.at[pl.ds(pl.multiple_of(source * rows[i], 8), rows[i]), :]

        arrivals, issued = [], 0
        for step in range(count):
            source = lax.rem(here - step + count, count)
            copies = []
            if step == 0:
                for i, whole_ref in enumerate(whole_refs):
                    copies.append((shard_refs[i], block(whole_ref, source, i)))
            else:
                for (group, _), part_ref in zip(parts, part_refs):
                    for slot, mask in enumerate(group):
                        target = piece ^ mask
                        start = 0
                        for i, (size, whole_ref) in enumerate(zip(sizes, whole_refs)):
                            if by_columns:
                                row = lax.rem(target, 4) * size
                                column = pl.ds(pl.multiple_of((target // 4) * width, 128), width)
                            else:
                                row, column = target * size, slice(None)
                            row = pl.multiple_of(source * rows[i] + row, 8)
                            copies.append(
                                (
                                    part_ref.at[slot, step - 1, start : start + size, :],
                                    whole_ref.at[pl.ds(row, size), column],
                                )
                            )
                            start += size
            made = []
            for origin, goal in copies:
                made.append(pltpu.make_async_copy(origin, goal, sems.at[issued]))
                made[-1].start()
                issued += 1
            arrivals.append((source, made))
        leaving = []
        for step, (source, made) in enumerate(arrivals):
            for copy in made:
                copy.wait()
            for i in range(many):
                leaving.append(
                    pltpu.make_async_copy(
                        block(whole_refs[i], source, i), block(out_refs[i], source, i), out_sems.at[step * many + i]
                    )
                )
                leaving[-1].start()
        for copy in leaving:
            copy.wait()

    total = sum(out.shape[0] * out.shape[1] * 2 for out in outs)
    return pl.pallas_call(
        kernel,
        out_shape=outs,
        in_specs=[pl.BlockSpec(memory_space=pltpu.SMEM)]
        + [pl.BlockSpec(memory_space=pl.ANY)] * (len(shards) + len(parts)),
        out_specs=[pl.BlockSpec(memory_space=pl.ANY)] * len(shards),
        scratch_shapes=[pltpu.VMEM(out.shape, out.dtype) for out in outs]
        + [
            pltpu.SemaphoreType.DMA((len(shards) * (1 + PIECES * (count - 1)),)),
            pltpu.SemaphoreType.DMA((len(shards) * count,)),
        ],
        name="assemble",
        compiler_params=pltpu.CompilerParams(vmem_limit_bytes=10 << 20),
        cost_estimate=pl.CostEstimate(flops=0, transcendentals=0, bytes_accessed=2 * total),
    )(jnp.stack([where, mine]).astype(jnp.int32), *shards, *[array for _, array in parts])


def send_round(piece):
    sent = [onward(piece, step) for step in range(1, lax.axis_size("shard"))]
    ring = jnp.stack(sent)
    return lax.optimization_barrier(ring)


def gather_direct(ring, token=None):
    got = [swap(ring, axes) for axes in ("xy", "x", "y")]
    if token is not None:
        ring = after(ring, token)
    near = jnp.stack([ring, got[1], got[2], got[0]])
    return (((0, 1, 2, 3), near), ((4, 5, 6, 7), swap(near, "c")))


def pick(value, index, axis):
    return lax.dynamic_index_in_dim(value, index, axis, keepdims=False)


def core_halves(value, blocks, axis=1):
    width = value.shape[axis] // blocks // 2

    def half(start):
        cut = [
            lax.slice_in_dim(value, (2 * j + start) * width, (2 * j + start + 1) * width, axis=axis)
            for j in range(blocks)
        ]
        return jnp.concatenate(cut, axis=axis)

    low, high = half(0), half(1)
    second = bit_of("c") == 1
    return jnp.where(second, high, low), jnp.where(second, low, high)


def add_low(*terms):
    total = terms[0].astype(jnp.float32)
    for term in terms[1:]:
        total = total + term.astype(jnp.float32)
    return total.astype(jnp.bfloat16)


def by_quarter(total):
    count = lax.axis_size("shard")
    rows, width = total.shape
    return total.reshape(count, 2, 2, rows // count // 4, width)


def sum_near(total, order):
    first, second = order
    for axis, dim in ((first, {"y": 1, "x": 2}[first]), (second, 1)):
        other = pick(total, 1 - bit_of(axis), dim)
        got = swap(other, axis)
        total = add_low(pick(total, bit_of(axis), dim), got)
    return total


def sum_near_direct(total):
    quarter = bit_of("y") * 2 + bit_of("x")
    total = total.reshape((total.shape[0], 4) + total.shape[3:])
    got = [swap(pick(total, quarter ^ mask, 1), axes) for mask, axes in ((3, "xy"), (1, "x"), (2, "y"))]
    return add_low(pick(total, quarter, 1), *got)


def sum_far(total):
    count = lax.axis_size("shard")
    here = lax.axis_index("shard")
    got = [onward(pick(total, (here + step) % count, 0), step) for step in range(1, count)]
    part = add_low(pick(total, here, 0), *got)
    extra = lax.axis_size("rep") // PIECES
    if extra > 1:
        groups = [[i + PIECES * j for j in range(extra)] for i in range(PIECES)]
        part = lax.psum(part, "rep", axis_index_groups=groups)
    return part


def share(part, outs, write, by_columns=False):
    size, width = part.shape
    got = [swap(part, axes) for axes in ("xy", "x", "y")]
    near = jnp.stack([part, got[1], got[2], got[0]])
    far = swap(near, "c")
    mine = bit_of("c") * 4 + bit_of("y") * 2 + bit_of("x")

    def kernel(mine_ref, near_ref, far_ref, *out_refs):
        here = pl.program_id(0) == mine_ref[0] // 4

        def lay(value_ref):
            for quarter in range(4):
                write(value_ref.at[(mine_ref[0] ^ quarter) % 4], *[out_ref.at[quarter] for out_ref in out_refs])

        @pl.when(here)
        def _():
            lay(near_ref)

        @pl.when(jnp.logical_not(here))
        def _():
            lay(far_ref)

    def goal(core, mine_ref):
        return (0, 0, core) if by_columns else (core, 0, 0)

    shapes = [
        jax.ShapeDtypeStruct((4, rows, 2 * columns) if by_columns else (8, rows, columns), kind)
        for (rows, columns), kind in outs
    ]
    return pl.pallas_call(
        kernel,
        grid_spec=pltpu.PrefetchScalarGridSpec(
            num_scalar_prefetch=1,
            grid=(2,),
            in_specs=[pl.BlockSpec((4, size, width), lambda core, mine_ref: (0, 0, 0))] * 2,
            out_specs=[pl.BlockSpec((4,) + shape, goal) for shape, _ in outs],
        ),
        out_shape=shapes,
        name="share",
        compiler_params=pltpu.CompilerParams(vmem_limit_bytes=28 << 20),
        cost_estimate=pl.CostEstimate(flops=0, transcendentals=0, bytes_accessed=32 * size * width),
    )(mine.astype(jnp.int32).reshape(1), near, far)


def turned(ref, start, cosine, sine_part, direction):
    half = DH // 2
    top, bottom = ref[start : start + half, :], ref[start + half : start + DH, :]
    return (
        top * cosine - direction * bottom * sine_part,
        bottom * cosine + direction * top * sine_part,
    )


FACTOR_ROWS = {"aq": 0, "ak": RQ * H, "av": (RQ + RK) * H, "bq": (RQ + 2 * RK) * H}
FACTOR_ROWS["bk"] = FACTOR_ROWS["bq"] + RQ * DH
FACTOR_ROWS["bv"] = FACTOR_ROWS["bk"] + RK * DH
SCORE_SCALE = DH**-0.5
LOG2E = math.log2(math.e)


def turn_all(factors_ref, cosine, sine_part, turned_ref):
    for slot in range(RQ + RK):
        top, bottom = turned(factors_ref, FACTOR_ROWS["bq"] + slot * DH, cosine, sine_part, 1.0)
        turned_ref[slot * DH : slot * DH + DH // 2, :] = top
        turned_ref[slot * DH + DH // 2 : (slot + 1) * DH, :] = bottom


def score_mask(length, rows):
    keys = lax.broadcasted_iota(jnp.int32, (rows, rows), 0)
    queries = lax.broadcasted_iota(jnp.int32, (rows, rows), 1)
    return jnp.where((keys <= queries) & (keys < length), 0.0, -1e30)


def contract(left, right, dims):
    return lax.dot_general(left, right, ((dims[:1], dims[1:]), ((), ())), preferred_element_type=jnp.float32)


def forward_kernel(
    length_ref, factors_ref, cosine_ref, sine_ref, out_ref, q_ref, k_ref, v_ref, lse_ref, turned_ref, mask_ref
):
    rows = factors_ref.shape[1]
    turn_all(factors_ref, cosine_ref[...], sine_ref[...], turned_ref)
    mask_ref[...] = score_mask(length_ref[pl.program_id(0)], rows)

    def mix(head, weight_row, base_ref, base_row, rank):
        total = None
        for r in range(rank):
            weight = factors_ref[pl.ds(weight_row + r * H + head, 1), :]
            term = weight * base_ref[base_row + r * DH : base_row + (r + 1) * DH, :]
            total = term if total is None else total + term
        return (total * (1.0 / rank)).astype(jnp.bfloat16)

    def one_head(head):
        span = pl.ds(pl.multiple_of(head * DH, DH), DH)
        query = mix(head, FACTOR_ROWS["aq"], turned_ref, 0, RQ)
        key = mix(head, FACTOR_ROWS["ak"], turned_ref, RQ * DH, RK)
        value = mix(head, FACTOR_ROWS["av"], factors_ref, FACTOR_ROWS["bv"], RK)
        q_ref[span, :] = query
        k_ref[span, :] = key
        v_ref[span, :] = value
        scores = contract(key, query, (0, 0)) + mask_ref[...]
        top = jnp.max(scores, axis=0, keepdims=True)
        shifted = jnp.exp2((scores - top) * (SCORE_SCALE * LOG2E))
        total = jnp.sum(shifted, axis=0, keepdims=True)
        lse_ref[pl.ds(head, 1), :] = top * SCORE_SCALE + jnp.log(total)
        probs = (shifted * (1.0 / total)).astype(jnp.bfloat16)
        out_ref[span, :] = contract(value, probs, (1, 0)).astype(jnp.bfloat16)

    @pl.loop(0, H // HEADS_AT_ONCE)
    def _(step):
        for j in range(HEADS_AT_ONCE):
            one_head(step * HEADS_AT_ONCE + j)


def backward_kernel(
    which, length_ref, factors_ref, cosine_ref, sine_ref, q_ref, k_ref, v_ref, lse_ref, grad_ref, *rest_refs
):
    out_ref, turned_ref, mask_ref, sums_ref, heads_ref = rest_refs[-5:]
    rows = factors_ref.shape[1]
    turn_all(factors_ref, cosine_ref[...], sine_ref[...], turned_ref)
    mask_ref[...] = score_mask(length_ref[which], rows)
    sums_ref[...] = jnp.zeros_like(sums_ref)

    def unmix(head, grad, weight_row, base_ref, base_row, sum_row, rank):
        for r in range(rank):
            weight = factors_ref[pl.ds(weight_row + r * H + head, 1), :]
            base = base_ref[base_row + r * DH : base_row + (r + 1) * DH, :]
            heads_ref[pl.ds(weight_row + r * H + head, 1), :] = jnp.sum(grad * base, axis=0, keepdims=True)
            sums_ref[sum_row + r * DH : sum_row + (r + 1) * DH, :] += grad * weight

    def one_head(head):
        span = pl.ds(pl.multiple_of(head * DH, DH), DH)
        query, key, value, grad = q_ref[span, :], k_ref[span, :], v_ref[span, :], grad_ref[span, :]
        scores = contract(key, query, (0, 0)) + mask_ref[...]
        lse = lse_ref[pl.ds(head, 1), :] * LOG2E
        probs = jnp.exp2(scores * (SCORE_SCALE * LOG2E) - lse)
        prob_grad = contract(value, grad, (0, 0))
        delta = jnp.sum(probs * prob_grad, axis=0, keepdims=True)
        score_grad = (probs * (prob_grad - delta)).astype(jnp.bfloat16)
        query_grad = contract(key, score_grad, (1, 0)) * (SCORE_SCALE / RQ)
        key_grad = contract(query, score_grad, (1, 1)) * (SCORE_SCALE / RK)
        value_grad = contract(grad, probs.astype(jnp.bfloat16), (1, 1)) * (1.0 / RK)
        unmix(head, query_grad, FACTOR_ROWS["aq"], turned_ref, 0, 0, RQ)
        unmix(head, key_grad, FACTOR_ROWS["ak"], turned_ref, RQ * DH, RQ * DH, RK)
        unmix(head, value_grad, FACTOR_ROWS["av"], factors_ref, FACTOR_ROWS["bv"], (RQ + RK) * DH, RK)

    @pl.loop(0, H // HEADS_AT_ONCE)
    def _(step):
        for j in range(HEADS_AT_ONCE):
            one_head(step * HEADS_AT_ONCE + j)

    low = jnp.bfloat16
    start = FACTOR_ROWS["bq"]
    out_ref[0:start, :] = heads_ref[...].astype(low)
    for slot in range(RQ + RK):
        top, bottom = turned(sums_ref, slot * DH, cosine_ref[...], sine_ref[...], -1.0)
        row = start + slot * DH
        out_ref[row : row + DH // 2, :] = top.astype(low)
        out_ref[row + DH // 2 : row + DH, :] = bottom.astype(low)
    row = FACTOR_ROWS["bv"]
    out_ref[row : row + RK * DH, :] = sums_ref[(RQ + RK) * DH :, :].astype(low)
    rest = out_ref.shape[0] - row - RK * DH
    out_ref[row + RK * DH :, :] = jnp.zeros((rest, rows), low)


HEADS_AT_ONCE = 2


def rotary_columns(seq_length):
    position = lax.iota(jnp.float32, seq_length)
    freq = jnp.exp(lax.iota(jnp.float32, DH // 2) * (-2.0 * math.log(10000.0) / DH))
    angle = freq[:, None] * position[None, :]
    return jnp.cos(angle), jnp.sin(angle)


def per_sequence(height, length):
    return pl.BlockSpec((height, length), lambda j: (0, j))


def attend(factors, lengths, tables):
    batches = lengths.shape[0]
    height, positions = factors.shape
    rows = positions // batches
    width = H * DH
    whole = pl.BlockSpec((DH // 2, rows), lambda j: (0, 0))
    flops = batches * H * rows * rows * DH * 2
    results = pl.pallas_call(
        forward_kernel,
        grid=(batches,),
        out_shape=[jax.ShapeDtypeStruct((width, positions), jnp.bfloat16)] * 4
        + [jax.ShapeDtypeStruct((H, positions), jnp.float32)],
        in_specs=[pl.BlockSpec(memory_space=pltpu.SMEM), per_sequence(height, rows), whole, whole],
        out_specs=[per_sequence(width, rows)] * 4 + [per_sequence(H, rows)],
        scratch_shapes=[
            pltpu.VMEM(((RQ + RK) * DH, rows), jnp.float32),
            pltpu.VMEM((rows, rows), jnp.float32),
        ],
        name="attend",
        compiler_params=pltpu.CompilerParams(vmem_limit_bytes=16 << 20),
            cost_estimate=pl.CostEstimate(
            flops=8 * flops, transcendentals=0, bytes_accessed=4 * height * positions + 8 * width * positions
        ),
    )(lengths, factors, *tables)
    return results[0], tuple(results[1:])


def attend_back(factors, lengths, tables, kept, grad):
    batches = lengths.shape[0]
    height, positions = factors.shape
    rows = positions // batches
    width = H * DH
    flops = H * rows * rows * DH * 2
    done = ()
    for which in range(batches):

        def one(height, which=which):
            return pl.BlockSpec((height, rows), lambda j: (0, which))

        whole = pl.BlockSpec((DH // 2, rows), lambda j: (0, 0))
        given = (lengths, factors, *tables, *kept, grad)
        done = (
            pl.pallas_call(
                functools.partial(backward_kernel, which),
                grid=(1,),
                out_shape=jax.ShapeDtypeStruct((height, positions), jnp.bfloat16),
                in_specs=[pl.BlockSpec(memory_space=pltpu.SMEM), one(height), whole, whole]
                + [one(width)] * 3
                + [one(H), one(width)]
                + [pl.BlockSpec(memory_space=pl.ANY)] * len(done),
                out_specs=one(height),
                scratch_shapes=[
                    pltpu.VMEM(((RQ + RK) * DH, rows), jnp.float32),
                    pltpu.VMEM((rows, rows), jnp.float32),
                    pltpu.VMEM(((RQ + 2 * RK) * DH, rows), jnp.float32),
                    pltpu.VMEM(((RQ + 2 * RK) * H, rows), jnp.float32),
                ],
                input_output_aliases={len(given): 0} if done else {},
                compiler_params=pltpu.CompilerParams(vmem_limit_bytes=16 << 20),
            cost_estimate=pl.CostEstimate(
                flops=20 * flops, transcendentals=0, bytes_accessed=6 * height * rows + 8 * width * rows
            ),
            )(*given, *done),
        )
    return done[0]


def matmul(left, right):
    return contract(left, right, (1, 0))


def matmul_back(left, right):
    return contract(left, right, (1, 1))


def norm_scale(value):
    return lax.rsqrt(jnp.mean(value * value, axis=-1, keepdims=True) + EPSILON)


def norm_back(grad, gain, normed, scale):
    scaled = grad * gain
    return scale * (scaled - normed * jnp.mean(scaled * normed, axis=-1, keepdims=True))


def deal(value):
    groups = lax.axis_size("shard")
    batches = value.shape[0] // groups
    rows, width = value.shape[1:]
    value = value.reshape(batches, groups, rows, width).swapaxes(0, 1)
    dealt = lax.all_to_all(value, "shard", split_axis=0, concat_axis=0, tiled=True)
    return dealt.swapaxes(0, 1).reshape(batches * groups * rows, width)


def give_back(value, batches):
    groups = lax.axis_size("shard")
    width = value.shape[-1]
    value = value.reshape(batches, groups, -1, width).swapaxes(0, 1)
    home = lax.all_to_all(value, "shard", split_axis=0, concat_axis=0, tiled=True)
    return home.swapaxes(0, 1).reshape(batches * groups, -1, width)


def on_device(
    tokens,
    cotangent,
    lengths,
    factor_weight,
    out_weight,
    gate_weight,
    up_weight,
    down_weight,
    first_gain,
    second_gain,
):
    low = jnp.bfloat16
    groups = lax.axis_size("shard")
    batches = tokens.shape[0] // groups
    row_count = tokens.shape[1] * groups
    factor_count = factor_weight.shape[1]
    padded = out_weight.shape[1]
    own_slot = lax.iota(jnp.int32, groups) == lax.axis_index("shard")
    own_lengths = jnp.sum(jnp.where(own_slot[None, :], lengths.reshape(batches, groups), 0), axis=1)
    live = (lax.iota(jnp.int32, row_count)[None, :] < own_lengths[:, None]).reshape(-1, 1)

    inputs = deal(tokens).astype(jnp.float32)
    shard = jnp.concatenate([factor_weight, first_gain[:, None], second_gain[:, None]], axis=1)
    shard = jnp.pad(shard, ((0, 0), (0, padded - factor_count - 2)))
    near_ring = send_round(jnp.concatenate([own_piece(shard), own_piece(out_weight)], axis=0))
    factor_full, out_full = assemble([shard, out_weight], gather_direct(near_ring))
    gate_parts = gather_direct(send_round(own_piece(gate_weight)))
    (gate_full,) = assemble([gate_weight], gate_parts)
    up_parts = gather_direct(send_round(own_piece(up_weight)))
    (up_full,) = assemble([up_weight], up_parts)
    down_ring = send_round(own_piece(down_weight, True))
    dealt_cotangent = deal(cotangent)

    at = lax.broadcasted_iota(jnp.int32, (8, padded), 1) - factor_count
    chosen = (at == lax.broadcasted_iota(jnp.int32, (8, padded), 0)).astype(low)
    last = factor_count // 128 * 128
    gains = matmul_back(chosen[:, last : last + 128], factor_full[:, last : last + 128])
    gain_one, gain_two = gains[0:1], gains[1:2]

    scale_one = norm_scale(inputs)
    normed_one = inputs * scale_one
    first_low = (normed_one * gain_one).astype(low)
    factors = contract(factor_full, first_low, (0, 1))
    tables = rotary_columns(row_count)
    attended, kept = attend(factors, own_lengths, tables)
    middle = inputs + contract(attended, out_full, (0, 0))
    scale_two = norm_scale(middle)
    normed_two = middle * scale_two
    second_low = (normed_two * gain_two).astype(low)
    gate_pre = lax.optimization_barrier(matmul(second_low, gate_full).astype(low)).astype(jnp.float32)
    up_pre = matmul(second_low, up_full)
    sigmoid = jax.nn.sigmoid(gate_pre)
    hidden = (gate_pre * sigmoid * up_pre).astype(low)
    up_pre = lax.optimization_barrier(up_pre.astype(low)).astype(jnp.float32)

    down_parts = gather_direct(down_ring, hidden)
    (down_full,) = assemble([down_weight], down_parts, True)
    upstream = jnp.where(live, after(dealt_cotangent, hidden).astype(jnp.float32), 0.0)
    upstream_low = upstream.astype(low)
    upstream_keep, upstream_send = core_halves(upstream_low, 1)
    down_send = contract(hidden, upstream_send, (0, 0)).astype(low)
    down_got = swap(down_send, "c")
    hidden_grad = matmul_back(after(upstream_low, down_send), down_full)
    gate_low = (hidden_grad * up_pre * sigmoid * (1.0 + gate_pre * (1.0 - sigmoid))).astype(low)
    up_low = (hidden_grad * gate_pre * sigmoid).astype(low)
    down_total = by_quarter(add_low(contract(hidden, after(upstream_keep, gate_low), (0, 0)), down_got))
    second_keep, second_send = core_halves(second_low, groups)
    gate_send = contract(after(second_send, down_total), gate_low, (0, 0)).astype(low)
    gate_got = swap(gate_send, "c")
    up_send = contract(after(second_send, gate_send), up_low, (0, 0)).astype(low)
    up_got = swap(up_send, "c")
    gate_total = by_quarter(add_low(contract(after(second_keep, up_send), gate_low, (0, 0)), gate_got))
    up_total = by_quarter(add_low(contract(after(second_keep, gate_total), up_low, (0, 0)), up_got))
    gate_low, up_low = lax.optimization_barrier((gate_low, up_low, up_total))[:2]
    second_in_grad = matmul_back(gate_low, gate_full) + matmul_back(up_low, up_full)
    second_gain_grad = jnp.sum(second_in_grad * normed_two, axis=0, keepdims=True)
    middle_grad = upstream + norm_back(second_in_grad, gain_two, normed_two, scale_two)
    middle_low = middle_grad.astype(low)
    attended_grad = matmul_back(out_full, middle_low).astype(low)
    attended_keep, attended_send = core_halves(attended, groups, 0)
    out_send = contract(attended_send, middle_low, (1, 0)).astype(low)
    out_got = swap(out_send, "c")
    out_total = by_quarter(add_low(contract(attended_keep, middle_low, (1, 0)), out_got))
    result = middle + matmul(after(hidden, out_send), down_full)
    output = jnp.where(live, result, 0.0).astype(low)
    home_output = give_back(output, batches)
    factor_low = attend_back(factors, own_lengths, tables, kept, after(attended_grad, output, out_total))

    gate_near = sum_near(gate_total, ("x", "y"))
    up_near = sum_near(up_total, ("y", "x"))
    pair_total = jnp.concatenate([gate_near, up_near], axis=1)
    first_in_grad = contract(after(factor_low, pair_total), factor_full, (0, 1))
    first_gain_grad = jnp.sum(first_in_grad * normed_one, axis=0, keepdims=True)
    input_grad = (
        middle_grad + norm_back(first_in_grad, gain_one, normed_one, scale_one)
    ).astype(low)
    home_grad = give_back(input_grad, batches)
    gain_rows = jnp.concatenate([first_gain_grad, second_gain_grad], axis=0)
    left = jnp.concatenate([first_low, jnp.pad(gain_rows, ((0, 126), (0, 0))).astype(low)], axis=0)
    right = jnp.concatenate([factor_low, jnp.pad(chosen.T, ((0, 0), (0, 120)))], axis=1)
    left_keep, left_send = core_halves(left, groups)
    factor_send = contract(left_send, right, (0, 1)).astype(low)
    factor_got = swap(factor_send, "c")
    factor_total = by_quarter(add_low(contract(left_keep, right, (0, 1)), factor_got))

    full = jnp.float32
    down_part = sum_far(sum_near(down_total, ("y", "x")))
    pair_part = sum_far(pair_total)
    near_total = [sum_near_direct(factor_total), sum_near_direct(out_total)]
    near_part = sum_far(jnp.concatenate(near_total, axis=1))

    def widen(value_ref, out_ref):
        out_ref[...] = value_ref[...].astype(full)

    def widen_pair(value_ref, gate_ref, up_ref):
        size = gate_ref.shape[0]
        gate_ref[...] = value_ref[:size, :].astype(full)
        up_ref[...] = value_ref[size:, :].astype(full)

    def widen_near(value_ref, factor_ref, out_ref):
        size = out_ref.shape[0]
        value = value_ref[...].astype(full)
        factor_ref[...] = value[:size]
        out_ref[...] = value[size:]

    (down_grad,) = share(down_part, [(down_part.shape, full)], widen, by_columns=True)
    size = gate_weight.shape[0] // PIECES
    block = (size, gate_weight.shape[1])
    gate_grad, up_grad = share(pair_part, [(block, full)] * 2, widen_pair)
    factor_grad, out_grad = share(near_part, [((size, padded), full)] * 2, widen_near)
    factor_grad = factor_grad.reshape(-1, padded)
    gain_sums = matmul_back(chosen[:, last : last + 128], factor_grad[:, last : last + 128].astype(low))
    return (
        home_output,
        home_grad,
        factor_grad[:, :factor_count],
        out_grad.reshape(out_weight.shape),
        gate_grad.reshape(gate_weight.shape),
        up_grad.reshape(up_weight.shape),
        down_grad.reshape(down_weight.shape),
        gain_sums[0],
        gain_sums[1],
    )


def solution(mesh):
    in_specs = (
        P("rep", "shard", None),
        P("rep", "shard", None),
        P("rep", None),
        P("shard", None),
        P("shard", None),
        P("shard", None),
        P("shard", None),
        P("shard", None),
        P("shard"),
        P("shard"),
    )
    out_specs = (
        P("rep", "shard", None),
        P("rep", "shard", None),
        P("shard", None),
        P("shard", None),
        P("shard", None),
        P("shard", None),
        P("shard", None),
        P("shard"),
        P("shard"),
    )
    return jax.shard_map(on_device, mesh=mesh, in_specs=in_specs, out_specs=out_specs, check_vma=False)
```
